32 devices in a mesh: groups: 2 (over y), ctx: 4 (over z), head: 2 (over x), qsub: 2 (over core).
Axes of the slice: x: 2, y: 2, z: 4, core: 2. Of those that a mesh axis runs over, the one named last changes fastest.
Arguments:
- queries: bfloat16 [4096, 2, 8, 128], P(('groups', 'ctx'), 'head', 'qsub'), parts along dimension 0, may hold values from -7 to 7
- key_states: bfloat16 [4096, 2, 128], P(('groups', 'ctx'), 'head'), parts along dimension 0, may hold values from -4 to 4
- value_states: bfloat16 [4096, 2, 128], P(('groups', 'ctx'), 'head'), parts along dimension 0, may hold values from -6 to 6
- block_table: int32 [16, 7], P(('groups', 'ctx')), parts along dimension 0, may hold values from -1 to 6, as said below
Outputs:
- attended: bfloat16 [4096, 2, 8, 128], P(('groups', 'ctx'), 'head', 'qsub'), parts along dimension 0
The draws below stay inside these ranges and needn't reach their ends.
There are 2 independent parts, one for each index of `groups`. The reference program is written for one: setup_inputs(seed, part) draws one part's arguments, and reference() takes and returns one part's arrays. A program takes and returns all parts, laid end to end along the dimension named above; each array names one. Nothing has to cross between parts.
Inputs may be any that keep to these rules, and one draw needn't show every extreme that they name: `block_table`: entry [b, k] is -1 or b - 2 ** k, and never below 0; it is b - 2 ** k wherever that value is 0 or 1, and in column 0 wherever b >= 1.
All inputs are finite; a program needn't handle non-finite values.
Results may differ from the reference program's by a relative error of at most 0.0044.
Values may be sent and summed in bfloat16 or wider, within the bound.
No kernel may reach another device: no remote copies, remote signals or barrier semaphores. Data moves between devices by JAX's collectives and lax.ppermute only.
A program may use at most 64 MiB of HBM per device.

```python
import jax
import jax.numpy as jnp
from jax import lax

DH = 128
QPK = 8
BLOCK = 256
SINKS = 4
LEVELS = 7
KVH = 2
TOKENS = 2048
NBLOCKS = 8


def draw_queries(key, part):
    full_shape = (TOKENS, KVH, QPK, DH)
    noise_key = jax.random.fold_in(key, 101)
    result = jnp.clip(jax.random.normal(noise_key, full_shape, jnp.float32), -4.0, 4.0)
    return result.astype(jnp.bfloat16)


def draw_key_states(key, part):
    full_shape = (TOKENS, KVH, DH)
    noise_key = jax.random.fold_in(key, 202)
    result = jnp.clip(jax.random.normal(noise_key, full_shape, jnp.float32), -4.0, 4.0)
    return result.astype(jnp.bfloat16)


def draw_block_table(key, part):
    block_position_index = jnp.arange(NBLOCKS, dtype=jnp.int32)[:, None]
    level_index = jnp.arange(LEVELS, dtype=jnp.int32)[None, :]
    distance = jnp.left_shift(jnp.ones_like(level_index), level_index)
    target_block = block_position_index - distance
    coin_toss = jax.random.randint(jax.random.fold_in(key, 303), (NBLOCKS, LEVELS), 0, 2)
    keep_entry = ((coin_toss > 0) | (level_index == 0) | (target_block < 2)) & (target_block >= 0)
    return jnp.where(keep_entry, target_block, -1).astype(jnp.int32)


def levels(rng, extent, split, smallest, high):
    factor_of = 1.0
    for axis_at, parts in split:
        draws = jax.random.uniform(jax.random.fold_in(jax.random.fold_in(rng, 6), axis_at), (parts,), jnp.float32, smallest / len(split), high / len(split))
        factor_of = factor_of * jnp.repeat(jnp.exp(draws), extent[axis_at] // parts).reshape((-1,) + (1,) * (len(extent) - 1 - axis_at))
    return factor_of


def scatter_about(rng, extent, scale, bound, cuts=(), held_as=jnp.bfloat16):
    gain = levels(rng, extent, cuts, -0.22, 0.18) if cuts else 1.0
    values = jax.random.normal(rng, extent, jnp.float32) * scale * gain
    return jnp.minimum(jnp.maximum(values, -bound), bound).astype(held_as)


def setup_inputs(seed: int = 0, part: int = 0) -> dict:
    seeds = jax.random.split(jax.random.key(seed), 5)
    part_splits = jax.random.split(jax.random.fold_in(seeds[4], part), 5)
    return {
        "queries": draw_queries(jax.random.fold_in(jax.random.fold_in(seeds[4], part), 71), part),
        "key_states": draw_key_states(jax.random.fold_in(jax.random.fold_in(seeds[4], part), 71), part),
        "value_states": scatter_about(part_splits[2], (TOKENS, KVH, DH), 1.0, 6.0, ((0, 4), (1, 2))),
        "block_table": draw_block_table(jax.random.fold_in(jax.random.fold_in(seeds[4], part), 71), part),
    }


def reference(queries, key_states, value_states, block_table):
    score_scale = DH ** -0.5
    slot_count = 1 + LEVELS + SINKS
    key_blocks = key_states.reshape(NBLOCKS, BLOCK, KVH, DH)
    value_blocks = value_states.reshape(NBLOCKS, BLOCK, KVH, DH)
    query_blocks = queries.reshape(NBLOCKS, BLOCK, KVH, QPK, DH)
    causal = jnp.arange(BLOCK)[:, None] >= jnp.arange(BLOCK)[None, :]
    local_masks = jnp.concatenate([causal[None], jnp.ones((slot_count - 1, BLOCK, BLOCK), bool)], axis=0)

    def attend_block(block_position_index):
        block_position_index = block_position_index.astype(jnp.int32)
        pattern_row = block_table[block_position_index]
        sink_ids = jnp.arange(SINKS, dtype=jnp.int32)
        named = jnp.any(pattern_row[None, :] == sink_ids[:, None], axis=1)
        slot_blocks = jnp.concatenate([block_position_index[None], jnp.maximum(pattern_row, 0).astype(jnp.int32), sink_ids]).astype(jnp.int32)
        slot_alive = jnp.concatenate([jnp.ones((1,), bool), pattern_row >= 0, (sink_ids < block_position_index) & (~named)])
        key_slots = key_blocks[slot_blocks].astype(jnp.float32)
        value_slots = value_blocks[slot_blocks].astype(jnp.float32)
        query_block = query_blocks[block_position_index].astype(jnp.float32)
        score_table = jnp.einsum('tgqd,sugd->gqtsu', query_block, key_slots) * score_scale
        allowed = (local_masks & slot_alive[:, None, None]).transpose(1, 0, 2)
        score_table = jnp.where(allowed[None, None], score_table, -1e30)
        highest = jnp.max(score_table, axis=(3, 4), keepdims=True)
        exponent = jnp.exp(score_table - highest)
        denominator = jnp.sum(exponent, axis=(3, 4))
        weights = lax.optimization_barrier(exponent.astype(jnp.bfloat16)).astype(jnp.float32)
        summed = jnp.einsum('gqtsu,sugd->tgqd', weights, value_slots)
        return (summed / denominator.transpose(2, 0, 1)[..., None]).astype(jnp.bfloat16)

    result_blocks = lax.map(attend_block, jnp.arange(NBLOCKS, dtype=jnp.int32))
    return result_blocks.reshape(TOKENS, KVH, QPK, DH)
```

```python
import functools
import math
from functools import reduce

import jax
import jax.numpy as jnp
from jax import lax
from jax.experimental import pallas as pl
from jax.experimental.pallas import tpu as pltpu
from jax.sharding import PartitionSpec as P

DH = 128
BLOCK = 256
SINKS = 4
LEVELS = 7
TILE = 256
STEP = 512
NEG = -1e30
BIG = 1e30
EXP2_SCALE = DH ** (-0.5) * math.log2(math.e)


def scores(q, k):
    return lax.dot_general(q, k, (((1,), (1,)), ((), ())), preferred_element_type=jnp.float32)


def update(q, items):
    raw, tops = [], []
    for k, _, counts, mask in items:
        s = scores(q, k)
        if mask is not None:
            s = jnp.where(mask, s, NEG)
        top = jnp.max(s, axis=1, keepdims=True)
        if counts is not None:
            top = jnp.where(counts, top, NEG)
        raw.append(s)
        tops.append(top)
    highest = reduce(jnp.maximum, tops)
    return raw, highest


def weighted(raw, items, highest):
    scaled = highest * EXP2_SCALE
    total = None
    for s, (_, v, counts, _) in zip(raw, items):
        shift = scaled if counts is None else jnp.where(counts, scaled, BIG)
        w = jnp.exp2(s * EXP2_SCALE - shift).astype(jnp.bfloat16)
        wide = jnp.concatenate([v, jnp.ones_like(v)], axis=1)
        part = jnp.dot(w, wide, preferred_element_type=jnp.float32)
        total = part if total is None else total + part
    return total


def named(table_ref, i, u):
    return reduce(lambda a, b: a | b, [table_ref[i, level] == u for level in range(LEVELS)])


def counts_of(kind, table_ref, i, block, u, first_here, blocks_here):
    before = (u >= 0) & (u < block)
    if kind == "here":
        return before & ((u < SINKS) | named(table_ref, i, u))
    elsewhere = (u < first_here) | (u >= first_here + blocks_here)
    if kind == "all":
        return before & elsewhere & ((u < SINKS) | named(table_ref, i, u))
    if kind == "sink":
        return before & elsewhere & (u < SINKS)
    return before & elsewhere & (u >= SINKS) & named(table_ref, i, u)


def stage(pieces, blocks_here, per_head, first, last, table_ref, q_ref, *refs):
    refs = list(refs)
    me = lax.axis_index("ctx")
    core = lax.axis_index("qsub")
    first_here = me * blocks_here
    steps_per_block = BLOCK * per_head // STEP
    i = pl.program_id(0) // steps_per_block
    within = pl.program_id(0) % steps_per_block
    block = first_here + i
    operands = []
    if first:
        k_ref, v_ref = refs.pop(0), refs.pop(0)
        for j in range(blocks_here - 1):
            span = pl.ds(j * BLOCK, BLOCK)
            counts = counts_of("here", table_ref, i, block, first_here + j, first_here, blocks_here)
            operands.append((k_ref, v_ref, (span,), counts))
    else:
        for kind, base, blocks in pieces:
            ref = refs.pop(0)
            start = base(me, core)
            for j in range(blocks):
                u = jnp.where(start < 0, -1, start + j)
                counts = counts_of(kind, table_ref, i, block, u, first_here, blocks_here)
                span = pl.ds(j * BLOCK, BLOCK)
                operands.append((ref.at[0], ref.at[1], (span,), counts))
        acc_in, stat_in = refs.pop(0), refs.pop(0)
    if last:
        (out_ref,) = refs
    else:
        acc_out, stat_out = refs
    lane = lax.broadcasted_iota(jnp.int32, (TILE, DH), 1)

    def finish(rows, acc, total, highest):
        if last:
            out_ref[rows, :] = (acc / total).astype(out_ref.dtype)
        else:
            acc_out[rows, :] = acc
            stat_out[rows, :] = jnp.where(lane < DH // 2, total, highest)

    def run(with_operands):
        for t in range(STEP // TILE):
            rows = pl.ds(t * TILE, TILE)
            items = []
            if first:
                own = pl.ds(pl.multiple_of(i * BLOCK, BLOCK), BLOCK)
                token = (
                    within * STEP + t * TILE + lax.broadcasted_iota(jnp.int32, (TILE, BLOCK), 0)
                ) // per_head
                mask = token >= lax.broadcasted_iota(jnp.int32, (TILE, BLOCK), 1)
                items.append((k_ref[own, :], v_ref[own, :], None, mask))
            if with_operands:
                for keys, values, span, counts in operands:
                    items.append((keys[span[0], :], values[span[0], :], counts, None))
            if not items:
                finish(rows, acc_in[rows, :], stat_in[rows, :1], stat_in[rows, DH // 2 : DH // 2 + 1])
                continue
            raw, highest = update(q_ref[rows, :], items)
            if not first:
                before = stat_in[rows, DH // 2 : DH // 2 + 1]
                highest = jnp.maximum(highest, before)
            sums = weighted(raw, items, highest)
            acc, total = sums[:, :DH], sums[:, DH:]
            if not first:
                keep = jnp.exp2((before - highest) * EXP2_SCALE)
                acc = acc + acc_in[rows, :] * keep
                total = total + stat_in[rows, :1] * keep
            finish(rows, acc, total, highest)

    if operands:
        some = reduce(lambda a, b: a | b, [o[3] for o in operands])
        pl.when(some)(lambda: run(True))
        pl.when(jnp.logical_not(some))(lambda: run(False))
    else:
        run(False)


def call_stage(pieces, arrays, blocks_here, per_head, table, q, state, last, name):
    first = state is None
    rows = q.shape[0]
    by_rows = lambda dtype: pl.BlockSpec((STEP, DH), lambda s: (s, 0))
    whole = lambda a: pl.BlockSpec(a.shape, lambda s, n=a.ndim: (0,) * n)
    in_specs = [pl.BlockSpec(memory_space=pltpu.SMEM), by_rows(q.dtype)]
    in_specs += [whole(a) for a in arrays]
    args = [table, q, *arrays]
    if not first:
        in_specs += [by_rows(jnp.float32)] * 2
        args += list(state)
    if last:
        out_shape = jax.ShapeDtypeStruct((rows, DH), q.dtype)
        out_specs = by_rows(q.dtype)
    else:
        out_shape = [jax.ShapeDtypeStruct((rows, DH), jnp.float32)] * 2
        out_specs = [by_rows(jnp.float32)] * 2
    keys = sum(a.size for a in arrays) // (2 * DH)
    return pl.pallas_call(
        functools.partial(stage, pieces, blocks_here, per_head, first, last),
        grid=(rows // STEP,),
        in_specs=in_specs,
        out_specs=out_specs,
        out_shape=out_shape,
        cost_estimate=pl.CostEstimate(
            flops=4 * rows * keys * DH, bytes_accessed=8 * rows * DH, transcendentals=rows * keys
        ),
        compiler_params=pltpu.CompilerParams(vmem_limit_bytes=24 << 20),
        name=name,
    )(*args)


def shards(queries, key_states, value_states, block_table):
    tokens = queries.shape[0]
    per_head = queries.shape[2]
    blocks_here = tokens // BLOCK
    context_count = lax.axis_size("ctx")
    cores = lax.axis_size("qsub")
    per_core = blocks_here // cores
    core = lax.axis_index("qsub")
    q = queries.reshape(tokens * per_head, DH)
    k = key_states.reshape(tokens, DH)
    v = value_states.reshape(tokens, DH)
    run = functools.partial(call_stage, blocks_here=blocks_here, per_head=per_head, table=block_table, q=q)

    part = per_core * BLOCK
    packed = jnp.stack(
        [lax.dynamic_slice_in_dim(k, core * part, part), lax.dynamic_slice_in_dim(v, core * part, part)]
    )

    def both_cores(arrived, kind, source):
        pieces, arrays = [], []
        for shift in range(cores):
            moved = arrived
            if shift:
                moved = lax.ppermute(arrived, "qsub", [(c, (c + shift) % cores) for c in range(cores)])
            base = lambda me, core, shift=shift: jnp.where(
                source(me) < 0, -1, source(me) * blocks_here + lax.rem(core - shift + cores, cores) * per_core
            )
            pieces.append((kind, base, per_core))
            arrays.append(moved)
        return pieces, arrays

    state = run([], [k, v], state=None, last=False, name="local")

    if context_count == 4:
        ring = [0, 1, 3, 2]
        after = {d: ring[(ring.index(d) + 1) % 4] for d in ring}
        before = {d: ring[(ring.index(d) - 1) % 4] for d in ring}
        look = lambda pairs: lambda me: reduce(
            lambda acc, d: jnp.where(me == d, pairs[d], acc), range(4), jnp.int32(0)
        )
        forward = [(d, after[d]) for d in range(4)]
        backward = [(d, before[d]) for d in range(4)]
        one = lax.ppermute(packed, "ctx", forward)
        held, state = lax.optimization_barrier((packed, state))
        back = lax.ppermute(held, "ctx", backward)
        two = lax.ppermute(one, "ctx", forward)
        arrivals = [
            (one, look(before)),
            (back, look(after)),
            (two, look({d: before[before[d]] for d in range(4)})),
        ]
        for n, (arrived, source) in enumerate(arrivals):
            pieces, arrays = both_cores(arrived, "all", source)
            state = run(pieces, arrays, state=state, last=n == 2, name=f"arrival_{n}")
        attended = state
    else:
        wanted = []
        for level in range(LEVELS):
            amount = max(2**level // blocks_here, 1)
            if amount < context_count and amount not in wanted:
                wanted.append(amount)
        roots = -(-SINKS // blocks_here)
        position = lax.axis_index("ctx")
        shared = [
            lax.psum(jnp.where(position == root, packed, jnp.zeros_like(packed)), "ctx") for root in range(roots)
        ]
        source_of = packed
        reached = 0
        stages = []
        for amount in wanted:
            hop = amount - reached
            source_of = lax.ppermute(source_of, "ctx", [(d, d + hop) for d in range(context_count - hop)])
            reached = amount
            stages.append(both_cores(source_of, "level", lambda me, amount=amount: jnp.maximum(me - amount, -1)))
        for root, arrived in enumerate(shared):
            stages.append(both_cores(arrived, "sink", lambda me, root=root: jnp.int32(root)))
        for n, (pieces, arrays) in enumerate(stages):
            state = run(pieces, arrays, state=state, last=n == len(stages) - 1, name=f"arrival_{n}")
        attended = state
    return attended.reshape(tokens, 1, per_head, DH)


def solution(mesh):
    placed = (
        P(("groups", "ctx"), "head", "qsub", None),
        P(("groups", "ctx"), "head", None),
        P(("groups", "ctx"), "head", None),
        P(("groups", "ctx"), None),
    )
    return jax.shard_map(
        shards,
        mesh=mesh,
        in_specs=placed,
        out_specs=P(("groups", "ctx"), "head", "qsub", None),
        check_vma=False,
    )
```

```python
import functools
import math
from functools import reduce

import jax
import jax.numpy as jnp
from jax import lax
from jax.experimental import pallas as pl
from jax.experimental.pallas import tpu as pltpu
from jax.sharding import PartitionSpec as P

DH = 128
BLOCK = 256
SINKS = 4
LEVELS = 7
TILE = 512
NEG = -1e30
BIG = 1e30
EXP2_SCALE = DH ** (-0.5) * math.log2(math.e)
ONES = 16


def named(table_ref, i, u):
    return reduce(lambda a, b: a | b, [table_ref[i, level] == u for level in range(LEVELS)])


def counts_of(kind, table_ref, i, block, u, first_here, blocks_here):
    before = (u >= 0) & (u < block)
    elsewhere = (u < first_here) | (u >= first_here + blocks_here)
    if kind == "all":
        return before & elsewhere & ((u < SINKS) | named(table_ref, i, u))
    if kind == "sink":
        return before & elsewhere & (u < SINKS)
    return before & elsewhere & (u >= SINKS) & named(table_ref, i, u)


def scores(k, q):
    return lax.dot_general(k, q, (((1,), (1,)), ((), ())), preferred_element_type=jnp.float32)


def widened(v, vt_ref):
    vt_ref[:DH, :] = v.T
    vt_ref[DH:, :] = jnp.ones((ONES, v.shape[0]), v.dtype)


def combine(q, items, before):
    raw, tops = [], [] if before is None else [before]
    for k, _, counts, mask in items:
        s = scores(k, q)
        if mask is not None:
            s = jnp.where(mask, s, NEG)
        top = jnp.max(s, axis=0, keepdims=True)
        raw.append(s)
        tops.append(top if counts is None else jnp.where(counts, top, NEG))
    highest = reduce(jnp.maximum, tops)
    scaled = highest * EXP2_SCALE
    total = None
    for s, (_, vt, counts, _) in zip(raw, items):
        shift = scaled if counts is None else jnp.where(counts, scaled, BIG)
        w = jnp.exp2(s * EXP2_SCALE - shift).astype(jnp.bfloat16)
        part = jnp.dot(vt, w, preferred_element_type=jnp.float32)
        total = part if total is None else total + part
    return total, highest


def keep_state(acc_ref, stat_ref, cols, acc, highest, total):
    acc_ref[:, cols] = acc
    stat_ref[:8, cols] = jnp.broadcast_to(highest, (8, TILE))
    stat_ref[8:, cols] = jnp.broadcast_to(total, (8, TILE))


def local_stage(per_head, cores, q_ref, *refs):
    refs = list(refs)
    parts = [refs.pop(0) for _ in range(cores)]
    table_ref = refs.pop(0) if len(refs) == 6 else None
    acc_ref, stat_ref, k_ref, v_ref, vt_ref = refs
    core = lax.axis_index("qsub")
    part = parts[0].shape[1]
    for shift, ref in enumerate(parts):
        at = pl.ds(pl.multiple_of(lax.rem(core - shift + cores, cores) * part, part), part)
        k_ref[at, :] = ref[0]
        v_ref[at, :] = ref[1]
    blocks_here = k_ref.shape[0] // BLOCK
    rows_per_block = BLOCK * per_head
    widened(v_ref[...], vt_ref)
    first_here = lax.axis_index("ctx") * blocks_here
    tokens = TILE // per_head
    for i in range(blocks_here):
        for t in range(rows_per_block // TILE):
            cols = pl.ds(i * rows_per_block + t * TILE, TILE)
            items = []
            for j in range(i):
                span = pl.ds(j * BLOCK, BLOCK)
                u = first_here + j
                counts = None if j == i - 1 else (u < SINKS) | named(table_ref, i, u)
                items.append((k_ref[span, :], vt_ref[:, span], counts, None))
            if t:
                span = pl.ds(i * BLOCK, t * tokens)
                items.append((k_ref[span, :], vt_ref[:, span], None, None))
            span = pl.ds(i * BLOCK + t * tokens, tokens)
            token = lax.broadcasted_iota(jnp.int32, (tokens, TILE), 1) // per_head
            mask = lax.broadcasted_iota(jnp.int32, (tokens, TILE), 0) <= token
            items.append((k_ref[span, :], vt_ref[:, span], None, mask))
            sums, highest = combine(q_ref[cols, :], items, None)
            keep_state(acc_ref, stat_ref, cols, sums[:DH], highest, sums[DH : DH + 8])


def arrival_stage(pieces, blocks_here, last, table_ref, q_ref, acc_in, stat_in, *refs):
    refs = list(refs)
    arrived = [refs.pop(0) for _ in pieces]
    if last:
        out_hbm, out_ref, vt_ref, sems = refs
    else:
        acc_ref, stat_ref, vt_ref = refs
    me, core = lax.axis_index("ctx"), lax.axis_index("qsub")
    first_here = me * blocks_here
    rows_per_block = q_ref.shape[0] // blocks_here
    blocks = []
    for (kind, base, count), ref in zip(pieces, arrived):
        start = base(me, core)
        for j in range(count):
            span = pl.ds(j * BLOCK, BLOCK)
            at = len(blocks)
            blocks.append((ref.at[0, span, :], vt_ref.at[at], kind, jnp.where(start < 0, -1, start + j), ref.at[1, span, :]))
    counts = [
        [counts_of(kind, table_ref, i, first_here + i, u, first_here, blocks_here) for _, _, kind, u, _ in blocks]
        for i in range(blocks_here)
    ]
    some = [reduce(lambda a, b: a | b, row) for row in counts]

    @pl.when(reduce(lambda a, b: a | b, some))
    def _():
        for _, vt, _, _, values in blocks:
            widened(values[...], vt)

    copies = []

    def finish(cols, acc, highest, total):
        if last:
            out_ref[cols, :] = (acc / total[:1]).astype(out_ref.dtype).T
        else:
            keep_state(acc_ref, stat_ref, cols, acc, highest, total)

    for i in range(blocks_here):
        tiles = [pl.ds(i * rows_per_block + t * TILE, TILE) for t in range(rows_per_block // TILE)]

        @pl.when(some[i])
        def _():
            for cols in tiles:
                items = [(k[...], vt[...], c, None) for (k, vt, _, _, _), c in zip(blocks, counts[i])]
                before = stat_in[:1, cols]
                sums, highest = combine(q_ref[cols, :], items, before)
                keep = jnp.exp2((before - highest) * EXP2_SCALE)
                finish(cols, acc_in[:, cols] * keep + sums[:DH], highest, stat_in[8:, cols] * keep + sums[DH : DH + 8])

        @pl.when(jnp.logical_not(some[i]))
        def _():
            for cols in tiles:
                finish(cols, acc_in[:, cols], stat_in[:1, cols], stat_in[8:, cols])

        if last:
            rows = pl.ds(i * rows_per_block, rows_per_block)
            copy = pltpu.make_async_copy(out_ref.at[rows], out_hbm.at[rows], sems.at[i])
            copy.start()
            copies.append(copy)
    for copy in copies:
        copy.wait()


VMEM_SPEC = pl.BlockSpec(memory_space=pltpu.VMEM)
ANY_SPEC = pl.BlockSpec(memory_space=pl.ANY)
PARAMS = pltpu.CompilerParams(vmem_limit_bytes=16 << 20)


def state_shapes(rows):
    return [jax.ShapeDtypeStruct((DH, rows), jnp.float32), jax.ShapeDtypeStruct((16, rows), jnp.float32)]


def cost(rows, keys):
    return pl.CostEstimate(flops=4 * rows * keys * DH, bytes_accessed=8 * rows * DH, transcendentals=rows * keys)


def call_local(q, parts, table, per_head):
    rows, tokens = q.shape[0], sum(a.shape[1] for a in parts)
    needs_table = tokens // BLOCK > 2
    return pl.pallas_call(
        functools.partial(local_stage, per_head, len(parts)),
        in_specs=[VMEM_SPEC] * (1 + len(parts)) + [pl.BlockSpec(memory_space=pltpu.SMEM)] * needs_table,
        out_specs=[VMEM_SPEC] * 2,
        out_shape=state_shapes(rows),
        scratch_shapes=[
            pltpu.VMEM((tokens, DH), q.dtype),
            pltpu.VMEM((tokens, DH), q.dtype),
            pltpu.VMEM((DH + ONES, tokens), q.dtype),
        ],
        cost_estimate=cost(rows, BLOCK),
        compiler_params=PARAMS,
        name="local",
    )(*([q, *parts] + [table] * needs_table))


def call_arrival(pieces, arrays, table, q, state, last, blocks_here, name):
    rows = q.shape[0]
    keys = sum(a.shape[1] for a in arrays)
    scratch = [pltpu.VMEM((keys // BLOCK, DH + ONES, BLOCK), q.dtype)]
    if last:
        scratch = [pltpu.VMEM(q.shape, q.dtype), *scratch, pltpu.SemaphoreType.DMA((blocks_here,))]
    return pl.pallas_call(
        functools.partial(arrival_stage, pieces, blocks_here, last),
        in_specs=[pl.BlockSpec(memory_space=pltpu.SMEM)] + [VMEM_SPEC] * (3 + len(arrays)),
        out_specs=ANY_SPEC if last else [VMEM_SPEC] * 2,
        out_shape=jax.ShapeDtypeStruct(q.shape, q.dtype) if last else state_shapes(rows),
        scratch_shapes=scratch,
        cost_estimate=cost(rows, keys),
        compiler_params=PARAMS,
        name=name,
    )(table, q, *state, *arrays)


def shards(queries, key_states, value_states, block_table):
    tokens = queries.shape[0]
    per_head = queries.shape[2]
    blocks_here = tokens // BLOCK
    context_count = lax.axis_size("ctx")
    cores = lax.axis_size("qsub")
    per_core = blocks_here // cores
    core = lax.axis_index("qsub")
    q = queries.reshape(tokens * per_head, DH)
    k = key_states.reshape(tokens, DH)
    v = value_states.reshape(tokens, DH)
    run = functools.partial(call_arrival, table=block_table, q=q, blocks_here=blocks_here)

    part = per_core * BLOCK
    packed = jnp.stack(
        [lax.dynamic_slice_in_dim(k, core * part, part), lax.dynamic_slice_in_dim(v, core * part, part)]
    )

    def swapped(arrived):
        return [arrived] + [
            lax.ppermute(arrived, "qsub", [(c, (c + shift) % cores) for c in range(cores)]) for shift in range(1, cores)
        ]

    def both_cores(arrived, kind, source):
        pieces = []
        for shift in range(cores):
            base = lambda me, core, shift=shift: jnp.where(
                source(me) < 0, -1, source(me) * blocks_here + lax.rem(core - shift + cores, cores) * per_core
            )
            pieces.append((kind, base, per_core))
        return pieces, swapped(arrived)

    if context_count == 4:
        ring = [0, 1, 3, 2]
        after = {d: ring[(ring.index(d) + 1) % 4] for d in ring}
        before = {d: ring[(ring.index(d) - 1) % 4] for d in ring}
        look = lambda pairs: lambda me: reduce(
            lambda acc, d: jnp.where(me == d, pairs[d], acc), range(4), jnp.int32(0)
        )
        forward = [(d, after[d]) for d in range(4)]
        backward = [(d, before[d]) for d in range(4)]
        one = lax.ppermute(packed, "ctx", backward)
        state = call_local(q, swapped(packed), block_table, per_head)
        held, one, state = lax.optimization_barrier((packed, one, state))
        other = lax.ppermute(held, "ctx", forward)
        two = lax.ppermute(one, "ctx", backward)
        arrivals = [
            (one, look(after)),
            (other, look(before)),
            (two, look({d: after[after[d]] for d in range(4)})),
        ]
        for n, (arrived, source) in enumerate(arrivals):
            if n:
                arrived = later[n - 1]
            pieces, arrays = both_cores(arrived, "all", source)
            state = run(pieces, arrays, state=state, last=n == 2, name=f"arrival_{n}")
            if n == 0:
                other, state = lax.optimization_barrier((other, state))
                two, state = lax.optimization_barrier((two, state))
                later = (other, two)
        attended = state
    else:
        state = call_local(q, swapped(packed), block_table, per_head)
        wanted = []
        for level in range(LEVELS):
            amount = max(2**level // blocks_here, 1)
            if amount < context_count and amount not in wanted:
                wanted.append(amount)
        roots = -(-SINKS // blocks_here)
        position = lax.axis_index("ctx")
        shared = [
            lax.psum(jnp.where(position == root, packed, jnp.zeros_like(packed)), "ctx") for root in range(roots)
        ]
        source_of = packed
        reached = 0
        stages = []
        for amount in wanted:
            hop = amount - reached
            source_of = lax.ppermute(source_of, "ctx", [(d, d + hop) for d in range(context_count - hop)])
            reached = amount
            stages.append(both_cores(source_of, "level", lambda me, amount=amount: jnp.maximum(me - amount, -1)))
        for root, arrived in enumerate(shared):
            stages.append(both_cores(arrived, "sink", lambda me, root=root: jnp.int32(root)))
        for n, (pieces, arrays) in enumerate(stages):
            state = run(pieces, arrays, state=state, last=n == len(stages) - 1, name=f"arrival_{n}")
        attended = state
    return attended.reshape(tokens, 1, per_head, DH)


def solution(mesh):
    placed = (
        P(("groups", "ctx"), "head", "qsub", None),
        P(("groups", "ctx"), "head", None),
        P(("groups", "ctx"), "head", None),
        P(("groups", "ctx"), None),
    )
    return jax.shard_map(
        shards,
        mesh=mesh,
        in_specs=placed,
        out_specs=P(("groups", "ctx"), "head", "qsub", None),
        check_vma=False,
    )
```

```python
import functools
import math
from functools import reduce

import jax
import jax.numpy as jnp
from jax import lax
from jax.experimental import pallas as pl
from jax.experimental.pallas import tpu as pltpu
from jax.sharding import PartitionSpec as P


DH = 128
BLOCK = 256
SINKS = 4
LEVELS = 7
TILE = 512
NEG = -1e30
BIG = 1e30
EXP2_SCALE = DH ** (-0.5) * math.log2(math.e)
ONES = 16


def named(table_ref, i, u):
    return reduce(lambda a, b: a | b, [table_ref[i, level] == u for level in range(LEVELS)])


def counts_of(kind, table_ref, i, block, u, first_here, blocks_here):
    before = (u >= 0) & (u < block)
    elsewhere = (u < first_here) | (u >= first_here + blocks_here)
    if kind == "all":
        return before & elsewhere & ((u < SINKS) | named(table_ref, i, u))
    if kind == "sink":
        return before & elsewhere & (u < SINKS)
    return before & elsewhere & (u >= SINKS) & named(table_ref, i, u)


def scores(k, q):
    return lax.dot_general(k, q, (((1,), (1,)), ((), ())), preferred_element_type=jnp.float32)


def widened(v, vt_ref):
    vt_ref[:DH, :] = v.T
    vt_ref[DH:, :] = jnp.ones((ONES, v.shape[0]), v.dtype)


def combine(q, items, before):
    raw, tops = [], [] if before is None else [before]
    for k, _, counts, mask in items:
        s = scores(k, q)
        if mask is not None:
            s = jnp.where(mask, s, NEG)
        top = jnp.max(s, axis=0, keepdims=True)
        raw.append(s)
        tops.append(top if counts is None else jnp.where(counts, top, NEG))
    highest = reduce(jnp.maximum, tops)
    scaled = highest * EXP2_SCALE
    total = None
    for s, (_, vt, counts, _) in zip(raw, items):
        shift = scaled if counts is None else jnp.where(counts, scaled, BIG)
        w = jnp.exp2(s * EXP2_SCALE - shift).astype(jnp.bfloat16)
        part = jnp.dot(vt, w, preferred_element_type=jnp.float32)
        total = part if total is None else total + part
    return total, highest


def keep_state(acc_ref, stat_ref, cols, acc, highest, total):
    acc_ref[:, cols] = acc
    stat_ref[:8, cols] = jnp.broadcast_to(highest, (8, TILE))
    stat_ref[8:, cols] = jnp.broadcast_to(total, (8, TILE))


def local_stage(per_head, cores, q_ref, *refs):
    refs = list(refs)
    parts = [refs.pop(0) for _ in range(cores)]
    table_ref = refs.pop(0) if len(refs) == 6 else None
    acc_ref, stat_ref, k_ref, v_ref, vt_ref = refs
    core = lax.axis_index("qsub")
    part = parts[0].shape[1]
    for shift, ref in enumerate(parts):
        at = pl.ds(pl.multiple_of(lax.rem(core - shift + cores, cores) * part, part), part)
        k_ref[at, :] = ref[0]
        v_ref[at, :] = ref[1]
    blocks_here = k_ref.shape[0] // BLOCK
    rows_per_block = BLOCK * per_head
    widened(v_ref[...], vt_ref)
    first_here = lax.axis_index("ctx") * blocks_here
    tokens = TILE // per_head
    for i in range(blocks_here):
        for t in range(rows_per_block // TILE):
            cols = pl.ds(i * rows_per_block + t * TILE, TILE)
            items = []
            for j in range(i):
                span = pl.ds(j * BLOCK, BLOCK)
                u = first_here + j
                counts = None if j == i - 1 else (u < SINKS) | named(table_ref, i, u)
                items.append((k_ref[span, :], vt_ref[:, span], counts, None))
            if t:
                span = pl.ds(i * BLOCK, t * tokens)
                items.append((k_ref[span, :], vt_ref[:, span], None, None))
            span = pl.ds(i * BLOCK + t * tokens, tokens)
            token = lax.broadcasted_iota(jnp.int32, (tokens, TILE), 1) // per_head
            mask = lax.broadcasted_iota(jnp.int32, (tokens, TILE), 0) <= token
            items.append((k_ref[span, :], vt_ref[:, span], None, mask))
            sums, highest = combine(q_ref[cols, :], items, None)
            keep_state(acc_ref, stat_ref, cols, sums[:DH], highest, sums[DH : DH + 8])


def flags_stage(stages, blocks_here, table_ref, flags_ref):
    me, core = lax.axis_index("ctx"), lax.axis_index("qsub")
    first_here = me * blocks_here
    for n, pieces in enumerate(stages):
        at = 0
        for kind, base, count in pieces:
            start = base(me, core)
            for j in range(count):
                u = jnp.where(start < 0, -1, start + j)
                for i in range(blocks_here):
                    counts = counts_of(kind, table_ref, i, first_here + i, u, first_here, blocks_here)
                    flags_ref[n, at] = counts.astype(jnp.int32)
                    at += 1


def arrival_stage(stage, operands, blocks_here, last, flags_ref, q_ref, acc_in, stat_in, *refs):
    refs = list(refs)
    arrived = [refs.pop(0) for _ in range(operands)]
    if last:
        out_hbm, out_ref, k_ref, vt_ref, sems = refs
    else:
        acc_ref, stat_ref, k_ref, vt_ref = refs
    rows_per_block = q_ref.shape[0] // blocks_here
    tiles = q_ref.shape[0] // TILE
    key_blocks = k_ref.shape[0] // BLOCK
    counts = [[flags_ref[stage, j * blocks_here + i] > 0 for j in range(key_blocks)] for i in range(blocks_here)]
    some = reduce(lambda a, b: a | b, sum(counts, []))

    def finish(t, acc, highest, total):
        cols = pl.ds(t * TILE, TILE)
        if not last:
            keep_state(acc_ref, stat_ref, cols, acc, highest, total)
            return
        out_ref[cols, :] = (acc / total[:1]).astype(out_ref.dtype).T
        pltpu.make_async_copy(out_ref.at[cols], out_hbm.at[cols], sems.at[t]).start()

    @pl.when(some)
    def _():
        at = 0
        for ref in arrived:
            span = pl.ds(at, ref.shape[1])
            k_ref[span, :] = ref[0]
            vt_ref[:DH, span] = ref[1].T
            at += ref.shape[1]
        vt_ref[DH:, :] = jnp.ones((ONES, at), vt_ref.dtype)
        k, vt = k_ref[...], vt_ref[...]
        raw = scores(k, q_ref[pl.ds(0, TILE), :])
        for t in range(tiles):
            s = raw
            if t + 1 < tiles:
                raw = scores(k, q_ref[pl.ds((t + 1) * TILE, TILE), :])
            cols = pl.ds(t * TILE, TILE)
            row = counts[t * TILE // rows_per_block]
            parts = [s[j * BLOCK : (j + 1) * BLOCK] for j in range(len(row))]
            tops = [jnp.where(c, jnp.max(part, axis=0, keepdims=True), NEG) for c, part in zip(row, parts)]
            before = stat_in[:1, cols]
            highest = reduce(jnp.maximum, tops, before)
            scaled = highest * EXP2_SCALE
            w = [jnp.exp2(part * EXP2_SCALE - jnp.where(c, scaled, BIG)).astype(vt.dtype) for c, part in zip(row, parts)]
            sums = jnp.dot(vt, jnp.concatenate(w, axis=0), preferred_element_type=jnp.float32)
            keep = jnp.exp2((before - highest) * EXP2_SCALE)
            finish(t, acc_in[:, cols] * keep + sums[:DH], highest, stat_in[8:, cols] * keep + sums[DH : DH + 8])

    @pl.when(jnp.logical_not(some))
    def _():
        for t in range(tiles):
            cols = pl.ds(t * TILE, TILE)
            finish(t, acc_in[:, cols], stat_in[:1, cols], stat_in[8:, cols])

    if last:
        for t in range(tiles):
            rows = pl.ds(t * TILE, TILE)
            pltpu.make_async_copy(out_ref.at[rows], out_hbm.at[rows], sems.at[t]).wait()


VMEM_SPEC = pl.BlockSpec(memory_space=pltpu.VMEM)
ANY_SPEC = pl.BlockSpec(memory_space=pl.ANY)
PARAMS = pltpu.CompilerParams(vmem_limit_bytes=16 << 20)


def state_shapes(rows):
    return [jax.ShapeDtypeStruct((DH, rows), jnp.float32), jax.ShapeDtypeStruct((16, rows), jnp.float32)]


def cost(rows, keys):
    return pl.CostEstimate(flops=4 * rows * keys * DH, bytes_accessed=8 * rows * DH, transcendentals=rows * keys)


def call_local(q, parts, table, per_head):
    rows, tokens = q.shape[0], sum(a.shape[1] for a in parts)
    needs_table = tokens // BLOCK > 2
    return pl.pallas_call(
        functools.partial(local_stage, per_head, len(parts)),
        in_specs=[VMEM_SPEC] * (1 + len(parts)) + [pl.BlockSpec(memory_space=pltpu.SMEM)] * needs_table,
        out_specs=[VMEM_SPEC] * 2,
        out_shape=state_shapes(rows),
        scratch_shapes=[
            pltpu.VMEM((tokens, DH), q.dtype),
            pltpu.VMEM((tokens, DH), q.dtype),
            pltpu.VMEM((DH + ONES, tokens), q.dtype),
        ],
        cost_estimate=cost(rows, BLOCK),
        compiler_params=PARAMS,
        name="local",
    )(*([q, *parts] + [table] * needs_table))


def call_flags(stages, table, blocks_here):
    entries = max(sum(count for _, _, count in pieces) for pieces in stages) * blocks_here
    return pl.pallas_call(
        functools.partial(flags_stage, stages, blocks_here),
        in_specs=[pl.BlockSpec(memory_space=pltpu.SMEM)],
        out_specs=pl.BlockSpec(memory_space=pltpu.SMEM),
        out_shape=jax.ShapeDtypeStruct((len(stages), entries), jnp.int32),
        compiler_params=PARAMS,
        name="flags",
    )(table)


def call_arrival(stage, arrays, flags, q, state, last, blocks_here):
    rows = q.shape[0]
    keys = sum(a.shape[1] for a in arrays)
    scratch = [pltpu.VMEM((keys, DH), q.dtype), pltpu.VMEM((DH + ONES, keys), q.dtype)]
    if last:
        scratch = [pltpu.VMEM(q.shape, q.dtype), *scratch, pltpu.SemaphoreType.DMA((rows // TILE,))]
    return pl.pallas_call(
        functools.partial(arrival_stage, stage, len(arrays), blocks_here, last),
        in_specs=[pl.BlockSpec(memory_space=pltpu.SMEM)] + [VMEM_SPEC] * (3 + len(arrays)),
        out_specs=ANY_SPEC if last else [VMEM_SPEC] * 2,
        out_shape=jax.ShapeDtypeStruct(q.shape, q.dtype) if last else state_shapes(rows),
        scratch_shapes=scratch,
        cost_estimate=cost(rows, keys),
        compiler_params=PARAMS,
    )(flags, q, *state, *arrays)


def shards(queries, key_states, value_states, block_table):
    tokens = queries.shape[0]
    per_head = queries.shape[2]
    blocks_here = tokens // BLOCK
    context_count = lax.axis_size("ctx")
    cores = lax.axis_size("qsub")
    per_core = blocks_here // cores
    core = lax.axis_index("qsub")
    q = queries.reshape(tokens * per_head, DH)
    k = key_states.reshape(tokens, DH)
    v = value_states.reshape(tokens, DH)
    run = functools.partial(call_arrival, q=q, blocks_here=blocks_here)

    part = per_core * BLOCK
    packed = jnp.stack(
        [lax.dynamic_slice_in_dim(k, core * part, part), lax.dynamic_slice_in_dim(v, core * part, part)]
    )

    def swapped(arrived):
        return [arrived] + [
            lax.ppermute(arrived, "qsub", [(c, (c + shift) % cores) for c in range(cores)]) for shift in range(1, cores)
        ]

    def pieces_of(kind, source):
        pieces = []
        for shift in range(cores):
            base = lambda me, core, shift=shift: jnp.where(
                source(me) < 0, -1, source(me) * blocks_here + lax.rem(core - shift + cores, cores) * per_core
            )
            pieces.append((kind, base, per_core))
        return pieces

    if context_count == 4:
        ring = [0, 1, 3, 2]
        after = {d: ring[(ring.index(d) + 1) % 4] for d in ring}
        before = {d: ring[(ring.index(d) - 1) % 4] for d in ring}
        look = lambda pairs: lambda me: reduce(
            lambda acc, d: jnp.where(me == d, pairs[d], acc), range(4), jnp.int32(0)
        )
        forward = [(d, after[d]) for d in range(4)]
        backward = [(d, before[d]) for d in range(4)]
        one = lax.ppermute(packed, "ctx", backward)
        state = call_local(q, swapped(packed), block_table, per_head)
        held, state = lax.optimization_barrier((packed, state))
        one, state = lax.optimization_barrier((one, state))
        other = lax.ppermute(held, "ctx", forward)
        two = lax.ppermute(one, "ctx", backward)
        sources = [look(after), look(before), look({d: after[after[d]] for d in range(4)})]
        flags = call_flags([pieces_of("all", source) for source in sources], block_table, blocks_here)
        arrivals = [one, other, two]
        for n in range(3):
            arrays = swapped(arrivals[n])
            state = run(n, arrays, flags, state=state, last=n == 2)
            if n == 0:
                other, state = lax.optimization_barrier((other, state))
                two, state = lax.optimization_barrier((two, state))
                arrivals = [one, other, two]
        attended = state
    else:
        state = call_local(q, swapped(packed), block_table, per_head)
        wanted = []
        for level in range(LEVELS):
            amount = max(2**level // blocks_here, 1)
            if amount < context_count and amount not in wanted:
                wanted.append(amount)
        roots = -(-SINKS // blocks_here)
        position = lax.axis_index("ctx")
        shared = [
            lax.psum(jnp.where(position == root, packed, jnp.zeros_like(packed)), "ctx") for root in range(roots)
        ]
        source_of = packed
        reached = 0
        stages = []
        for amount in wanted:
            hop = amount - reached
            source_of = lax.ppermute(source_of, "ctx", [(d, d + hop) for d in range(context_count - hop)])
            reached = amount
            stages.append((source_of, pieces_of("level", lambda me, amount=amount: jnp.maximum(me - amount, -1))))
        for root, arrived in enumerate(shared):
            stages.append((arrived, pieces_of("sink", lambda me, root=root: jnp.int32(root))))
        flags = call_flags([pieces for _, pieces in stages], block_table, blocks_here)
        for n, (arrived, _) in enumerate(stages):
            state = run(n, swapped(arrived), flags, state=state, last=n == len(stages) - 1)
        attended = state
    return attended.reshape(tokens, 1, per_head, DH)


def solution(mesh):
    placed = (
        P(("groups", "ctx"), "head", "qsub", None),
        P(("groups", "ctx"), "head", None),
        P(("groups", "ctx"), "head", None),
        P(("groups", "ctx"), None),
    )

    return jax.shard_map(
        shards,
        mesh=mesh,
        in_specs=placed,
        out_specs=P(("groups", "ctx"), "head", "qsub", None),
        check_vma=False,
    )
```

```python
import functools
import math
from functools import reduce

import jax
import jax.numpy as jnp
from jax import lax
from jax.experimental import pallas as pl
from jax.experimental.pallas import tpu as pltpu
from jax.sharding import PartitionSpec as P


DH = 128
BLOCK = 256
SINKS = 4
LEVELS = 7
TILE = 512
NEG = -1e30
BIG = 1e30
EXP2_SCALE = DH ** (-0.5) * math.log2(math.e)
ONES = 16


def named(table_ref, i, u):
    return reduce(lambda a, b: a | b, [table_ref[i, level] == u for level in range(LEVELS)])


def counts_of(kind, table_ref, i, block, u, first_here, blocks_here):
    before = (u >= 0) & (u < block)
    elsewhere = (u < first_here) | (u >= first_here + blocks_here)
    if kind == "all":
        return before & elsewhere & ((u < SINKS) | named(table_ref, i, u))
    if kind == "sink":
        return before & elsewhere & (u < SINKS)
    return before & elsewhere & (u >= SINKS) & named(table_ref, i, u)


def scores(k, q):
    return lax.dot_general(k, q, (((1,), (1,)), ((), ())), preferred_element_type=jnp.float32)


def top_of(s):
    return jnp.max(s, axis=0, keepdims=True)


def weights(s, shift):
    return jnp.exp2(s * EXP2_SCALE - shift).astype(jnp.bfloat16)


def keep_state(acc_ref, stat_ref, cols, acc, highest, total):
    acc_ref[:, cols] = acc
    stat_ref[:8, cols] = jnp.broadcast_to(highest, (8, TILE))
    stat_ref[8:, cols] = total


def local_stage(i, per_head, cores, q_ref, *refs):
    refs = list(refs)
    parts = [refs.pop(0) for _ in range(cores)]
    table_ref = refs.pop(0) if len(refs) == 6 else None
    acc_ref, stat_ref, k_ref, v_ref, vt_ref = refs
    core = lax.axis_index("qsub")
    part = parts[0].shape[1]
    for shift, ref in enumerate(parts):
        at = pl.ds(pl.multiple_of(lax.rem(core - shift + cores, cores) * part, part), part)
        k_ref[at, :] = ref[0]
        v_ref[at, :] = ref[1]
    keys = (i + 1) * BLOCK
    vt_ref[:DH, :] = v_ref[:keys, :].T
    vt_ref[DH:, :] = jnp.ones((ONES, keys), vt_ref.dtype)
    rows_per_block = BLOCK * per_head
    tokens = TILE // per_head
    first_here = lax.axis_index("ctx") * (k_ref.shape[0] // BLOCK)
    for t in range(rows_per_block // TILE):
        q = q_ref[pl.ds(i * rows_per_block + t * TILE, TILE), :]
        edge = i * BLOCK + t * tokens
        items = []
        for j in range(i):
            s = scores(k_ref[pl.ds(j * BLOCK, BLOCK), :], q)
            if j < i - 1:
                u = first_here + j
                s = jnp.where((u < SINKS) | named(table_ref, i, u), s, NEG)
            items.append(s)
        if t:
            items.append(scores(k_ref[pl.ds(i * BLOCK, t * tokens), :], q))
        token = lax.broadcasted_iota(jnp.int32, (tokens, TILE), 1) // per_head
        mask = lax.broadcasted_iota(jnp.int32, (tokens, TILE), 0) <= token
        items.append(jnp.where(mask, scores(k_ref[pl.ds(edge, tokens), :], q), NEG))
        highest = reduce(jnp.maximum, [top_of(s) for s in items])
        w = jnp.concatenate([weights(s, highest * EXP2_SCALE) for s in items], axis=0)
        sums = jnp.dot(vt_ref[:, : edge + tokens], w, preferred_element_type=jnp.float32)
        keep_state(acc_ref, stat_ref, pl.ds(t * TILE, TILE), sums[:DH], highest, sums[DH : DH + 8])


def flags_stage(stages, blocks_here, table_ref, flags_ref):
    me, core = lax.axis_index("ctx"), lax.axis_index("qsub")
    first_here = me * blocks_here
    at = 0
    for pieces in stages:
        for kind, base, count in pieces:
            start = base(me, core)
            for j in range(count):
                u = jnp.where(start < 0, -1, start + j)
                for i in range(blocks_here):
                    counts = counts_of(kind, table_ref, i, first_here + i, u, first_here, blocks_here)
                    flags_ref[at : at + 1, :] = jnp.full((1, TILE), jnp.where(counts, 0.0, BIG), jnp.float32)
                    at += 1


def arrival_stage(source, row_of, operands, blocks_here, last, *refs):
    refs = list(refs)
    flags_ref = None if row_of is None else refs.pop(0)
    q_ref = refs.pop(0)
    state_in = [(refs.pop(0), refs.pop(0)) for _ in range(blocks_here)]
    arrived = [refs.pop(0) for _ in range(operands)]
    if last:
        out_hbm, out_ref, k_ref, vt_ref, sems = refs
    else:
        state_out = [(refs.pop(0), refs.pop(0)) for _ in range(blocks_here)]
        k_ref, vt_ref = refs
    me = lax.axis_index("ctx")
    origin = source(me)
    some = (origin >= 0) & (origin < me)
    per_block = q_ref.shape[0] // blocks_here // TILE
    tiles = per_block * blocks_here
    key_blocks = k_ref.shape[0] // BLOCK

    def finish(t, acc, highest, total):
        if not last:
            keep_state(*state_out[t // per_block], pl.ds(t % per_block * TILE, TILE), acc, highest, total)
            return
        rows = pl.ds(t * TILE, TILE)
        out_ref[rows, :] = (acc / total[:1]).astype(out_ref.dtype).T
        pltpu.make_async_copy(out_ref.at[rows], out_hbm.at[rows], sems.at[t]).start()

    @pl.when(some)
    def _():
        at = 0
        for ref in arrived:
            span = pl.ds(at, ref.shape[1])
            k_ref[span, :] = ref[0]
            vt_ref[:DH, span] = ref[1].T
            at += ref.shape[1]
        vt_ref[DH:, :] = jnp.ones((ONES, at), vt_ref.dtype)
        k, vt = k_ref[...], vt_ref[...]
        raw = scores(k, q_ref[pl.ds(0, TILE), :])
        for t in range(tiles):
            s = raw
            if t + 1 < tiles:
                raw = scores(k, q_ref[pl.ds((t + 1) * TILE, TILE), :])
            i, cols = t // per_block, pl.ds(t % per_block * TILE, TILE)
            acc_in, stat_in = state_in[i]
            before = stat_in[:1, cols]
            if row_of is None:
                highest = jnp.maximum(before, top_of(s))
                w = weights(s, highest * EXP2_SCALE)
            else:
                parts = [s[j * BLOCK : (j + 1) * BLOCK] for j in range(key_blocks)]
                at = [row_of + j * blocks_here + i for j in range(key_blocks)]
                off = [flags_ref[n : n + 1, :] for n in at]
                highest = reduce(jnp.maximum, [top_of(part) - o for part, o in zip(parts, off)], before)
                scaled = highest * EXP2_SCALE
                w = jnp.concatenate([weights(part, scaled + o) for part, o in zip(parts, off)], axis=0)
            sums = jnp.dot(vt, w, preferred_element_type=jnp.float32)
            keep = jnp.exp2((before - highest) * EXP2_SCALE)
            finish(t, acc_in[:, cols] * keep + sums[:DH], highest, stat_in[8:, cols] * keep + sums[DH : DH + 8])

    @pl.when(jnp.logical_not(some))
    def _():
        for t in range(tiles):
            cols = pl.ds(t % per_block * TILE, TILE)
            acc_in, stat_in = state_in[t // per_block]
            finish(t, acc_in[:, cols], stat_in[:1, cols], stat_in[8:, cols])

    if last:
        for t in range(tiles):
            rows = pl.ds(t * TILE, TILE)
            pltpu.make_async_copy(out_ref.at[rows], out_hbm.at[rows], sems.at[t]).wait()


VMEM_SPEC = pl.BlockSpec(memory_space=pltpu.VMEM)
SMEM_SPEC = pl.BlockSpec(memory_space=pltpu.SMEM)
ANY_SPEC = pl.BlockSpec(memory_space=pl.ANY)
PARAMS = pltpu.CompilerParams(vmem_limit_bytes=16 << 20)


def state_shapes(rows):
    return [jax.ShapeDtypeStruct((DH, rows), jnp.float32), jax.ShapeDtypeStruct((16, rows), jnp.float32)]


def cost(rows, keys):
    return pl.CostEstimate(flops=4 * rows * keys * DH, bytes_accessed=8 * rows * DH, transcendentals=rows * keys)


def call_local(i, q, parts, table, per_head):
    tokens = sum(a.shape[1] for a in parts)
    rows = BLOCK * per_head
    needs_table = i > 1
    return pl.pallas_call(
        functools.partial(local_stage, i, per_head, len(parts)),
        in_specs=[VMEM_SPEC] * (1 + len(parts)) + [SMEM_SPEC] * needs_table,
        out_specs=[VMEM_SPEC] * 2,
        out_shape=state_shapes(rows),
        scratch_shapes=[
            pltpu.VMEM((tokens, DH), q.dtype),
            pltpu.VMEM((tokens, DH), q.dtype),
            pltpu.VMEM((DH + ONES, (i + 1) * BLOCK), q.dtype),
        ],
        cost_estimate=cost(rows, (i + 1) * BLOCK),
        compiler_params=PARAMS,
    )(*([q, *parts] + [table] * needs_table))


def call_flags(stages, table, blocks_here):
    entries = sum(count for pieces in stages for _, _, count in pieces) * blocks_here
    return pl.pallas_call(
        functools.partial(flags_stage, stages, blocks_here),
        in_specs=[SMEM_SPEC],
        out_specs=VMEM_SPEC,
        out_shape=jax.ShapeDtypeStruct((-(-entries // 8) * 8, TILE), jnp.float32),
        compiler_params=PARAMS,
        name="flags",
    )(table)


def call_arrival(source, row_of, arrays, flags, q, state, last=False):
    rows = q.shape[0]
    keys = sum(a.shape[1] for a in arrays)
    scratch = [pltpu.VMEM((keys, DH), q.dtype), pltpu.VMEM((DH + ONES, keys), q.dtype)]
    if last:
        scratch = [pltpu.VMEM(q.shape, q.dtype), *scratch, pltpu.SemaphoreType.DMA((rows // TILE,))]
    args = [] if row_of is None else [flags]
    args += [q, *[a for pair in state for a in pair], *arrays]
    out = pl.pallas_call(
        functools.partial(arrival_stage, source, row_of, len(arrays), len(state), last),
        in_specs=[VMEM_SPEC] * len(args),
        out_specs=ANY_SPEC if last else [VMEM_SPEC] * (2 * len(state)),
        out_shape=jax.ShapeDtypeStruct(q.shape, q.dtype) if last else state_shapes(rows // len(state)) * len(state),
        scratch_shapes=scratch,
        cost_estimate=cost(rows, keys),
        compiler_params=PARAMS,
    )(*args)
    return out if last else [(out[2 * i], out[2 * i + 1]) for i in range(len(state))]


def shards(queries, key_states, value_states, block_table):
    tokens = queries.shape[0]
    per_head = queries.shape[2]
    blocks_here = tokens // BLOCK
    context_count = lax.axis_size("ctx")
    cores = lax.axis_size("qsub")
    per_core = blocks_here // cores
    core = lax.axis_index("qsub")
    q = queries.reshape(tokens * per_head, DH)
    k = key_states.reshape(tokens, DH)
    v = value_states.reshape(tokens, DH)

    part = per_core * BLOCK
    packed = jnp.stack(
        [lax.dynamic_slice_in_dim(k, core * part, part), lax.dynamic_slice_in_dim(v, core * part, part)]
    )

    def swapped(arrived):
        return [
            lax.ppermute(arrived, "qsub", [(c, (c + shift) % cores) for c in range(cores)])
            for shift in range(1, cores)
        ]

    def hop(block, route):
        return lax.ppermute(block, "ctx", route)

    def local(i, parts):
        return call_local(i, q, parts, block_table, per_head)

    def pieces_of(kind, source):
        pieces = []
        for shift in range(cores):
            base = lambda me, core, shift=shift: jnp.where(
                source(me) < 0, -1, source(me) * blocks_here + lax.rem(core - shift + cores, cores) * per_core
            )
            pieces.append((kind, base, per_core))
        return pieces

    def flags_of(stages):
        return call_flags(stages, block_table, blocks_here)

    if context_count == 4:
        ring = [0, 1, 3, 2]
        after = {d: ring[(ring.index(d) + 1) % 4] for d in ring}
        before = {d: ring[(ring.index(d) - 1) % 4] for d in ring}
        forward = [(d, after[d]) for d in range(4)]
        backward = [(d, before[d]) for d in range(4)]
        origins = [after, before, {d: after[after[d]] for d in range(4)}]
        sources = [
            lambda me, pairs=pairs: reduce(lambda acc, d: jnp.where(me == d, pairs[d], acc), range(4), jnp.int32(0))
            for pairs in origins
        ]
        tabled = [any(o < d and (o + 1) * blocks_here > SINKS for d, o in pairs.items()) for pairs in origins]
        row_of, listed = [], []
        for n in range(3):
            row_of.append(len(listed) * per_core * cores * blocks_here if tabled[n] else None)
            if tabled[n]:
                listed.append(pieces_of("all", sources[n]))

        one = hop(packed, backward)
        parts = [packed, *swapped(packed)]
        state = [local(0, parts)]
        held, state[0] = lax.optimization_barrier((packed, state[0]))
        other = hop(held, forward)
        flags = flags_of(listed) if listed else None
        state += [local(i, parts) for i in range(1, blocks_here)]
        one, state = lax.optimization_barrier((one, state))
        swap = swapped(one)
        two = hop(one, backward)
        state = call_arrival(sources[0], row_of[0], [one, *swap], flags, q, state)
        for n, arrived in ((1, other), (2, two)):
            arrived, state = lax.optimization_barrier((arrived, state))
            swap = swapped(arrived)
            row = row_of[n]
            state = call_arrival(sources[n], row, [arrived], flags, q, state)
            row = None if row is None else row + per_core * blocks_here
            state = call_arrival(sources[n], row, swap, flags, q, state, last=n == 2)
        attended = state
    else:
        parts = [packed, *swapped(packed)]
        state = [local(i, parts) for i in range(blocks_here)]
        wanted = []
        for level in range(LEVELS):
            amount = max(2**level // blocks_here, 1)
            if amount < context_count and amount not in wanted:
                wanted.append(amount)
        roots = -(-SINKS // blocks_here)
        position = lax.axis_index("ctx")
        shared = [
            lax.psum(jnp.where(position == root, packed, jnp.zeros_like(packed)), "ctx") for root in range(roots)
        ]
        stages = []
        moved, reached = packed, 0
        for amount in wanted:
            step = amount - reached
            moved = hop(moved, [(d, d + step) for d in range(context_count - step)])
            reached = amount
            stages.append((moved, "level", lambda me, amount=amount: jnp.maximum(me - amount, -1)))
        for root, arrived in enumerate(shared):
            stages.append((arrived, "sink", lambda me, root=root: jnp.int32(root)))
        flags = flags_of([pieces_of(kind, source) for _, kind, source in stages])
        for n, (arrived, _, source) in enumerate(stages):
            row = n * per_core * cores * blocks_here
            arrays = [arrived, *swapped(arrived)]
            state = call_arrival(source, row, arrays, flags, q, state, last=n == len(stages) - 1)
        attended = state
    return attended.reshape(tokens, 1, per_head, DH)


def solution(mesh):
    placed = (
        P(("groups", "ctx"), "head", "qsub", None),
        P(("groups", "ctx"), "head", None),
        P(("groups", "ctx"), "head", None),
        P(("groups", "ctx"), None),
    )

    return jax.shard_map(
        shards,
        mesh=mesh,
        in_specs=placed,
        out_specs=P(("groups", "ctx"), "head", "qsub", None),
        check_vma=False,
    )
```

```python
import functools
import math
from functools import reduce

import jax
import jax.numpy as jnp
from jax import lax
from jax.experimental import pallas as pl
from jax.experimental.pallas import tpu as pltpu
from jax.sharding import PartitionSpec as P


DH = 128
BLOCK = 256
SINKS = 4
LEVELS = 7
TILE = 512
NEG = -1e30
BIG = 1e30
EXP2_SCALE = DH ** (-0.5) * math.log2(math.e)
ONES = 16


def named(table_ref, i, u):
    return reduce(lambda a, b: a | b, [table_ref[i, level] == u for level in range(LEVELS)])


def counts_of(kind, table_ref, i, block, u, first_here, blocks_here):
    before = (u >= 0) & (u < block)
    elsewhere = (u < first_here) | (u >= first_here + blocks_here)
    if kind == "all":
        return before & elsewhere & ((u < SINKS) | named(table_ref, i, u))
    if kind == "sink":
        return before & elsewhere & (u < SINKS)
    return before & elsewhere & (u >= SINKS) & named(table_ref, i, u)


def scores(k, q):
    return lax.dot_general(k, q, (((1,), (1,)), ((), ())), preferred_element_type=jnp.float32)


def top_of(s):
    return jnp.max(s, axis=0, keepdims=True)


def weights(s, shift):
    return jnp.exp2(s * EXP2_SCALE - shift).astype(jnp.bfloat16)


def keep_state(acc_ref, stat_ref, cols, acc, highest, total):
    acc_ref[:, cols] = acc
    stat_ref[:8, cols] = jnp.broadcast_to(highest, (8, TILE))
    stat_ref[8:, cols] = total


def local_stage(i, per_head, cores, q_ref, *refs):
    refs = list(refs)
    parts = [refs.pop(0) for _ in range(cores)]
    table_ref = refs.pop(0) if len(refs) == 6 else None
    acc_ref, stat_ref, k_ref, v_ref, vt_ref = refs
    core = lax.axis_index("qsub")
    part = parts[0].shape[1]
    for shift, ref in enumerate(parts):
        at = pl.ds(pl.multiple_of(lax.rem(core - shift + cores, cores) * part, part), part)
        k_ref[at, :] = ref[0]
        v_ref[at, :] = ref[1]
    keys = (i + 1) * BLOCK
    vt_ref[:DH, :] = v_ref[:keys, :].T
    vt_ref[DH:, :] = jnp.ones((ONES, keys), vt_ref.dtype)
    rows_per_block = BLOCK * per_head
    tokens = TILE // per_head
    first_here = lax.axis_index("ctx") * (k_ref.shape[0] // BLOCK)
    for t in range(rows_per_block // TILE):
        q = q_ref[pl.ds(i * rows_per_block + t * TILE, TILE), :]
        edge = i * BLOCK + t * tokens
        items = []
        for j in range(i):
            s = scores(k_ref[pl.ds(j * BLOCK, BLOCK), :], q)
            if j < i - 1:
                u = first_here + j
                s = jnp.where((u < SINKS) | named(table_ref, i, u), s, NEG)
            items.append(s)
        if t:
            items.append(scores(k_ref[pl.ds(i * BLOCK, t * tokens), :], q))
        token = lax.broadcasted_iota(jnp.int32, (tokens, TILE), 1) // per_head
        mask = lax.broadcasted_iota(jnp.int32, (tokens, TILE), 0) <= token
        items.append(jnp.where(mask, scores(k_ref[pl.ds(edge, tokens), :], q), NEG))
        highest = reduce(jnp.maximum, [top_of(s) for s in items])
        w = jnp.concatenate([weights(s, highest * EXP2_SCALE) for s in items], axis=0)
        sums = jnp.dot(vt_ref[:, : edge + tokens], w, preferred_element_type=jnp.float32)
        keep_state(acc_ref, stat_ref, pl.ds(t * TILE, TILE), sums[:DH], highest, sums[DH : DH + 8])


def flags_stage(stages, blocks_here, table_ref, flags_ref):
    me, core = lax.axis_index("ctx"), lax.axis_index("qsub")
    first_here = me * blocks_here
    at = 0
    for pieces in stages:
        for kind, base, count in pieces:
            start = base(me, core)
            for j in range(count):
                u = jnp.where(start < 0, -1, start + j)
                for i in range(blocks_here):
                    counts = counts_of(kind, table_ref, i, first_here + i, u, first_here, blocks_here)
                    flags_ref[at : at + 1, :] = jnp.full((1, TILE), jnp.where(counts, 0.0, BIG), jnp.float32)
                    at += 1


def arrival_stage(source, row_of, operands, blocks_here, last, *refs):
    refs = list(refs)
    flags_ref = None if row_of is None else refs.pop(0)
    q_ref = refs.pop(0)
    state_in = [(refs.pop(0), refs.pop(0)) for _ in range(blocks_here)]
    arrived = [refs.pop(0) for _ in range(operands)]
    if last:
        out_hbm, out_ref, k_ref, vt_ref, sems = refs
    else:
        state_out = [(refs.pop(0), refs.pop(0)) for _ in range(blocks_here)]
        k_ref, vt_ref = refs
    me = lax.axis_index("ctx")
    origin = source(me)
    some = (origin >= 0) & (origin < me)
    per_block = q_ref.shape[0] // blocks_here // TILE
    tiles = per_block * blocks_here
    key_blocks = k_ref.shape[0] // BLOCK

    def finish(t, acc, highest, total):
        if not last:
            keep_state(*state_out[t // per_block], pl.ds(t % per_block * TILE, TILE), acc, highest, total)
            return
        rows = pl.ds(t * TILE, TILE)
        out_ref[rows, :] = (acc * (1.0 / total[:1])).astype(out_ref.dtype).T
        pltpu.make_async_copy(out_ref.at[rows], out_hbm.at[rows], sems.at[t]).start()

    @pl.when(some)
    def _():
        at = 0
        for ref in arrived:
            span = pl.ds(at, ref.shape[1])
            k_ref[span, :] = ref[0]
            vt_ref[:DH, span] = ref[1].T
            at += ref.shape[1]
        vt_ref[DH:, :] = jnp.ones((ONES, at), vt_ref.dtype)
        k, vt = k_ref[...], vt_ref[...]
        raw = scores(k, q_ref[pl.ds(0, TILE), :])
        for t in range(tiles):
            s = raw
            if t + 1 < tiles:
                raw = scores(k, q_ref[pl.ds((t + 1) * TILE, TILE), :])
            i, cols = t // per_block, pl.ds(t % per_block * TILE, TILE)
            acc_in, stat_in = state_in[i]
            before = stat_in[:1, cols]
            if row_of is None:
                highest = jnp.maximum(before, top_of(s))
                w = weights(s, highest * EXP2_SCALE)
            else:
                parts = [s[j * BLOCK : (j + 1) * BLOCK] for j in range(key_blocks)]
                at = [row_of + j * blocks_here + i for j in range(key_blocks)]
                off = [flags_ref[n : n + 1, :] for n in at]
                highest = reduce(jnp.maximum, [top_of(part) - o for part, o in zip(parts, off)], before)
                scaled = highest * EXP2_SCALE
                w = jnp.concatenate([weights(part, scaled + o) for part, o in zip(parts, off)], axis=0)
            sums = jnp.dot(vt, w, preferred_element_type=jnp.float32)
            keep = jnp.exp2((before - highest) * EXP2_SCALE)
            finish(t, acc_in[:, cols] * keep + sums[:DH], highest, stat_in[8:, cols] * keep + sums[DH : DH + 8])

    @pl.when(jnp.logical_not(some))
    def _():
        for t in range(tiles):
            cols = pl.ds(t % per_block * TILE, TILE)
            acc_in, stat_in = state_in[t // per_block]
            finish(t, acc_in[:, cols], stat_in[:1, cols], stat_in[8:, cols])

    if last:
        for t in range(tiles):
            rows = pl.ds(t * TILE, TILE)
            pltpu.make_async_copy(out_ref.at[rows], out_hbm.at[rows], sems.at[t]).wait()


VMEM_SPEC = pl.BlockSpec(memory_space=pltpu.VMEM)
SMEM_SPEC = pl.BlockSpec(memory_space=pltpu.SMEM)
ANY_SPEC = pl.BlockSpec(memory_space=pl.ANY)
PARAMS = pltpu.CompilerParams(vmem_limit_bytes=16 << 20)


def state_shapes(rows):
    return [jax.ShapeDtypeStruct((DH, rows), jnp.float32), jax.ShapeDtypeStruct((16, rows), jnp.float32)]


def cost(rows, keys):
    return pl.CostEstimate(flops=4 * rows * keys * DH, bytes_accessed=8 * rows * DH, transcendentals=rows * keys)


def call_local(i, q, parts, table, per_head):
    tokens = sum(a.shape[1] for a in parts)
    rows = BLOCK * per_head
    needs_table = i > 1
    return pl.pallas_call(
        functools.partial(local_stage, i, per_head, len(parts)),
        in_specs=[VMEM_SPEC] * (1 + len(parts)) + [SMEM_SPEC] * needs_table,
        out_specs=[VMEM_SPEC] * 2,
        out_shape=state_shapes(rows),
        scratch_shapes=[
            pltpu.VMEM((tokens, DH), q.dtype),
            pltpu.VMEM((tokens, DH), q.dtype),
            pltpu.VMEM((DH + ONES, (i + 1) * BLOCK), q.dtype),
        ],
        cost_estimate=cost(rows, (i + 1) * BLOCK),
        compiler_params=PARAMS,
    )(*([q, *parts] + [table] * needs_table))


def call_flags(stages, table, blocks_here):
    entries = sum(count for pieces in stages for _, _, count in pieces) * blocks_here
    return pl.pallas_call(
        functools.partial(flags_stage, stages, blocks_here),
        in_specs=[SMEM_SPEC],
        out_specs=VMEM_SPEC,
        out_shape=jax.ShapeDtypeStruct((-(-entries // 8) * 8, TILE), jnp.float32),
        compiler_params=PARAMS,
        name="flags",
    )(table)


def call_arrival(source, row_of, arrays, flags, q, state, last=False):
    rows = q.shape[0]
    keys = sum(a.shape[1] for a in arrays)
    scratch = [pltpu.VMEM((keys, DH), q.dtype), pltpu.VMEM((DH + ONES, keys), q.dtype)]
    if last:
        scratch = [pltpu.VMEM(q.shape, q.dtype), *scratch, pltpu.SemaphoreType.DMA((rows // TILE,))]
    args = [] if row_of is None else [flags]
    args += [q, *[a for pair in state for a in pair], *arrays]
    out = pl.pallas_call(
        functools.partial(arrival_stage, source, row_of, len(arrays), len(state), last),
        in_specs=[VMEM_SPEC] * len(args),
        out_specs=ANY_SPEC if last else [VMEM_SPEC] * (2 * len(state)),
        out_shape=jax.ShapeDtypeStruct(q.shape, q.dtype) if last else state_shapes(rows // len(state)) * len(state),
        scratch_shapes=scratch,
        cost_estimate=cost(rows, keys),
        compiler_params=PARAMS,
    )(*args)
    return out if last else [(out[2 * i], out[2 * i + 1]) for i in range(len(state))]


def shards(queries, key_states, value_states, block_table):
    tokens = queries.shape[0]
    per_head = queries.shape[2]
    blocks_here = tokens // BLOCK
    context_count = lax.axis_size("ctx")
    cores = lax.axis_size("qsub")
    per_core = blocks_here // cores
    core = lax.axis_index("qsub")
    q = queries.reshape(tokens * per_head, DH)
    k = key_states.reshape(tokens, DH)
    v = value_states.reshape(tokens, DH)

    part = per_core * BLOCK
    packed = jnp.stack(
        [lax.dynamic_slice_in_dim(k, core * part, part), lax.dynamic_slice_in_dim(v, core * part, part)]
    )

    def swapped(arrived):
        return [
            lax.ppermute(arrived, "qsub", [(c, (c + shift) % cores) for c in range(cores)])
            for shift in range(1, cores)
        ]

    def hop(block, route):
        return lax.ppermute(block, "ctx", route)

    def local(i, parts):
        return call_local(i, q, parts, block_table, per_head)

    def pieces_of(kind, source):
        pieces = []
        for shift in range(cores):
            base = lambda me, core, shift=shift: jnp.where(
                source(me) < 0, -1, source(me) * blocks_here + lax.rem(core - shift + cores, cores) * per_core
            )
            pieces.append((kind, base, per_core))
        return pieces

    def flags_of(stages):
        return call_flags(stages, block_table, blocks_here)

    if context_count == 4:
        ring = [0, 1, 2, 3]
        after = {d: ring[(ring.index(d) + 1) % 4] for d in ring}
        before = {d: ring[(ring.index(d) - 1) % 4] for d in ring}
        forward = [(d, after[d]) for d in range(4)]
        backward = [(d, before[d]) for d in range(4)]
        origins = [before, after, {0: 3, 1: 2, 2: 0, 3: 1}]
        sources = [
            lambda me, pairs=pairs: reduce(lambda acc, d: jnp.where(me == d, pairs[d], acc), range(4), jnp.int32(0))
            for pairs in origins
        ]
        tabled = [any(o < d and (o + 1) * blocks_here > SINKS for d, o in pairs.items()) for pairs in origins]
        row_of, listed = [], []
        for n in range(3):
            row_of.append(len(listed) * per_core * cores * blocks_here if tabled[n] else None)
            if tabled[n]:
                listed.append(pieces_of("all", sources[n]))

        one = hop(packed, forward)
        parts = [packed, *swapped(packed)]
        state = [local(0, parts)]
        held, state[0] = lax.optimization_barrier((packed, state[0]))
        other = hop(held, backward)
        flags = flags_of(listed) if listed else None
        state += [local(i, parts) for i in range(1, blocks_here)]
        one, state = lax.optimization_barrier((one, state))
        swap = swapped(one)
        route = [(c, (c + 1) % cores) for c in range(cores)]
        route += [(a * cores + c, b * cores + c) for a, b in ((1, 2), (2, 3), (3, 1)) for c in range(cores)]
        two = lax.ppermute(one, ("ctx", "qsub"), route)
        state = call_arrival(sources[0], row_of[0], [one, *swap], flags, q, state)
        for n, arrived in ((1, other), (2, two)):
            arrived, state = lax.optimization_barrier((arrived, state))
            swap = swapped(arrived)
            row = row_of[n]
            state = call_arrival(sources[n], row, [arrived], flags, q, state)
            row = None if row is None else row + per_core * blocks_here
            state = call_arrival(sources[n], row, swap, flags, q, state, last=n == 2)
        attended = state
    else:
        parts = [packed, *swapped(packed)]
        state = [local(i, parts) for i in range(blocks_here)]
        wanted = []
        for level in range(LEVELS):
            amount = max(2**level // blocks_here, 1)
            if amount < context_count and amount not in wanted:
                wanted.append(amount)
        roots = -(-SINKS // blocks_here)
        position = lax.axis_index("ctx")
        shared = [
            lax.psum(jnp.where(position == root, packed, jnp.zeros_like(packed)), "ctx") for root in range(roots)
        ]
        stages = []
        moved, reached = packed, 0
        for amount in wanted:
            step = amount - reached
            moved = hop(moved, [(d, d + step) for d in range(context_count - step)])
            reached = amount
            stages.append((moved, "level", lambda me, amount=amount: jnp.maximum(me - amount, -1)))
        for root, arrived in enumerate(shared):
            stages.append((arrived, "sink", lambda me, root=root: jnp.int32(root)))
        flags = flags_of([pieces_of(kind, source) for _, kind, source in stages])
        for n, (arrived, _, source) in enumerate(stages):
            row = n * per_core * cores * blocks_here
            arrays = [arrived, *swapped(arrived)]
            state = call_arrival(source, row, arrays, flags, q, state, last=n == len(stages) - 1)
        attended = state
    return attended.reshape(tokens, 1, per_head, DH)


def solution(mesh):
    placed = (
        P(("groups", "ctx"), "head", "qsub", None),
        P(("groups", "ctx"), "head", None),
        P(("groups", "ctx"), "head", None),
        P(("groups", "ctx"), None),
    )

    return jax.shard_map(
        shards,
        mesh=mesh,
        in_specs=placed,
        out_specs=P(("groups", "ctx"), "head", "qsub", None),
        check_vma=False,
    )
```

```python
import functools
import math
from functools import reduce

import jax
import jax.numpy as jnp
from jax import lax
from jax.experimental import pallas as pl
from jax.experimental.pallas import tpu as pltpu
from jax.sharding import PartitionSpec as P


DH = 128
BLOCK = 256
SINKS = 4
LEVELS = 7
TILE = 512
NEG = -1e30
BIG = 1e30
EXP2_SCALE = DH ** (-0.5) * math.log2(math.e)
ONES = 16


def named(table_ref, i, u):
    return reduce(lambda a, b: a | b, [table_ref[i, level] == u for level in range(LEVELS)])


def counts_of(kind, table_ref, i, block, u, first_here, blocks_here):
    before = (u >= 0) & (u < block)
    elsewhere = (u < first_here) | (u >= first_here + blocks_here)
    if kind == "all":
        return before & elsewhere & ((u < SINKS) | named(table_ref, i, u))
    if kind == "sink":
        return before & elsewhere & (u < SINKS)
    return before & elsewhere & (u >= SINKS) & named(table_ref, i, u)


def split_queries(q):
    scaled = q.astype(jnp.float32) * EXP2_SCALE
    high = scaled.astype(jnp.bfloat16)
    low = (scaled - high.astype(jnp.float32)).astype(jnp.bfloat16)
    return jnp.concatenate([high, low], axis=1)


def scores(k, q):
    return lax.dot_general(k, q, (((1,), (1,)), ((), ())), preferred_element_type=jnp.float32)


def top_of(s):
    return jnp.max(s, axis=0, keepdims=True)


def weights(s, shift):
    return jnp.exp2(s - shift).astype(jnp.bfloat16)


def keep_state(acc_ref, stat_ref, cols, acc, highest, total):
    acc_ref[:, cols] = acc
    stat_ref[:8, cols] = jnp.broadcast_to(highest, total.shape)
    stat_ref[8:, cols] = total


def local_stage(i, per_head, cores, q_ref, *refs):
    refs = list(refs)
    parts = [refs.pop(0) for _ in range(cores)]
    table_ref = refs.pop(0) if len(refs) == 7 else None
    acc_ref, stat_ref, split_ref, k_ref, v_ref, vt_ref = refs
    core = lax.axis_index("qsub")
    part = parts[0].shape[1]
    for shift, ref in enumerate(parts):
        at = pl.ds(pl.multiple_of(lax.rem(core - shift + cores, cores) * part, part), part)
        k_ref[at, :DH] = ref[0]
        k_ref[at, DH:] = ref[0]
        v_ref[at, :] = ref[1]
    keys = (i + 1) * BLOCK
    vt_ref[:DH, :] = v_ref[:keys, :].T
    vt_ref[DH:, :] = jnp.ones((ONES, keys), vt_ref.dtype)
    rows_per_block = BLOCK * per_head
    tokens = TILE // per_head
    first_here = lax.axis_index("ctx") * (k_ref.shape[0] // BLOCK)
    for t in range(rows_per_block // TILE):
        q = split_queries(q_ref[pl.ds(i * rows_per_block + t * TILE, TILE), :])
        split_ref[pl.ds(t * TILE, TILE), :] = q
        edge = i * BLOCK + t * tokens
        items = []
        for j in range(i):
            s = scores(k_ref[pl.ds(j * BLOCK, BLOCK), :], q)
            if j < i - 1:
                u = first_here + j
                s = jnp.where((u < SINKS) | named(table_ref, i, u), s, NEG)
            items.append(s)
        if t:
            items.append(scores(k_ref[pl.ds(i * BLOCK, t * tokens), :], q))
        token = lax.broadcasted_iota(jnp.int32, (tokens, TILE), 1) // per_head
        mask = lax.broadcasted_iota(jnp.int32, (tokens, TILE), 0) <= token
        items.append(jnp.where(mask, scores(k_ref[pl.ds(edge, tokens), :], q), NEG))
        highest = reduce(jnp.maximum, [top_of(s) for s in items])
        w = jnp.concatenate([weights(s, highest) for s in items], axis=0)
        sums = jnp.dot(vt_ref[:, : edge + tokens], w, preferred_element_type=jnp.float32)
        keep_state(acc_ref, stat_ref, pl.ds(t * TILE, TILE), sums[:DH], highest, sums[DH : DH + 8])


def flags_stage(stages, blocks_here, table_ref, flags_ref):
    me, core = lax.axis_index("ctx"), lax.axis_index("qsub")
    first_here = me * blocks_here
    at = 0
    for pieces in stages:
        for kind, base, count in pieces:
            start = base(me, core)
            for j in range(count):
                u = jnp.where(start < 0, -1, start + j)
                for i in range(blocks_here):
                    counts = counts_of(kind, table_ref, i, first_here + i, u, first_here, blocks_here)
                    flags_ref[at : at + 1, :] = jnp.full((1, TILE), jnp.where(counts, 0.0, BIG), jnp.float32)
                    at += 1


def arrival_stage(source, row_of, operands, blocks_here, last, *refs):
    refs = list(refs)
    flags_ref = None if row_of is None else refs.pop(0)
    state_in = [(refs.pop(0), refs.pop(0), refs.pop(0)) for _ in range(blocks_here)]
    arrived = [refs.pop(0) for _ in range(operands)]
    if last:
        out_hbm, out_ref, k_ref, vt_ref, sems = refs
    else:
        state_out = [(refs.pop(0), refs.pop(0)) for _ in range(blocks_here)]
        k_ref, vt_ref = refs
    me = lax.axis_index("ctx")
    origin = source(me)
    some = (origin >= 0) & (origin < me)
    key_blocks = k_ref.shape[0] // BLOCK
    rows_per_block = state_in[0][0].shape[1]
    tile = min(TILE, k_ref.shape[0])
    depth = 2 * TILE // tile
    per_block = rows_per_block // tile
    tiles = per_block * blocks_here

    def place(t):
        return t // per_block, pl.ds(t % per_block * tile, tile)

    def finish(t, acc, highest, total):
        i, cols = place(t)
        if not last:
            keep_state(*state_out[i], cols, acc, highest, total)
            return
        rows = pl.ds(t * tile, tile)
        out_ref[rows, :] = (acc * (1.0 / total[:1])).astype(out_ref.dtype).T
        pltpu.make_async_copy(out_ref.at[rows], out_hbm.at[rows], sems.at[t]).start()

    @pl.when(some)
    def _():
        at = 0
        for ref in arrived:
            span = pl.ds(at, ref.shape[1])
            k_ref[span, :DH] = ref[0]
            k_ref[span, DH:] = ref[0]
            vt_ref[:DH, span] = ref[1].T
            at += ref.shape[1]
        vt_ref[DH:, :] = jnp.ones((ONES, at), vt_ref.dtype)
        k, vt = k_ref[...], vt_ref[...]

        def begin(t):
            i, cols = place(t)
            return scores(k, state_in[i][2][cols, :])

        raw = [begin(t) for t in range(min(depth, tiles))]
        for t in range(tiles):
            if t + depth < tiles:
                raw.append(begin(t + depth))
            s = raw.pop(0)
            i, cols = place(t)
            acc_in, stat_in, _ = state_in[i]
            before = stat_in[:1, cols]
            if row_of is None:
                highest = jnp.maximum(before, top_of(s))
                w = weights(s, highest)
            else:
                parts = [s[j * BLOCK : (j + 1) * BLOCK] for j in range(key_blocks)]
                at = [row_of + j * blocks_here + i for j in range(key_blocks)]
                off = [flags_ref[n : n + 1, :tile] for n in at]
                highest = reduce(jnp.maximum, [top_of(part) - o for part, o in zip(parts, off)], before)
                w = jnp.concatenate([weights(part, highest + o) for part, o in zip(parts, off)], axis=0)
            sums = jnp.dot(vt, w, preferred_element_type=jnp.float32)
            keep = jnp.exp2(before - highest)
            finish(t, acc_in[:, cols] * keep + sums[:DH], highest, stat_in[8:, cols] * keep + sums[DH : DH + 8])

    @pl.when(jnp.logical_not(some))
    def _():
        for t in range(tiles):
            i, cols = place(t)
            acc_in, stat_in, _ = state_in[i]
            finish(t, acc_in[:, cols], stat_in[:1, cols], stat_in[8:, cols])

    if last:
        for t in range(tiles):
            rows = pl.ds(t * tile, tile)
            pltpu.make_async_copy(out_ref.at[rows], out_hbm.at[rows], sems.at[t]).wait()


VMEM_SPEC = pl.BlockSpec(memory_space=pltpu.VMEM)
SMEM_SPEC = pl.BlockSpec(memory_space=pltpu.SMEM)
ANY_SPEC = pl.BlockSpec(memory_space=pl.ANY)
PARAMS = pltpu.CompilerParams(vmem_limit_bytes=16 << 20)


def state_shapes(rows):
    return [jax.ShapeDtypeStruct((DH, rows), jnp.float32), jax.ShapeDtypeStruct((16, rows), jnp.float32)]


def cost(rows, keys):
    return pl.CostEstimate(flops=4 * rows * keys * DH, bytes_accessed=8 * rows * DH, transcendentals=rows * keys)


def call_local(i, q, parts, table, per_head):
    tokens = sum(a.shape[1] for a in parts)
    rows = BLOCK * per_head
    needs_table = i > 1
    return pl.pallas_call(
        functools.partial(local_stage, i, per_head, len(parts)),
        in_specs=[VMEM_SPEC] * (1 + len(parts)) + [SMEM_SPEC] * needs_table,
        out_specs=[VMEM_SPEC] * 3,
        out_shape=[*state_shapes(rows), jax.ShapeDtypeStruct((rows, 2 * DH), q.dtype)],
        scratch_shapes=[
            pltpu.VMEM((tokens, 2 * DH), q.dtype),
            pltpu.VMEM((tokens, DH), q.dtype),
            pltpu.VMEM((DH + ONES, (i + 1) * BLOCK), q.dtype),
        ],
        cost_estimate=cost(rows, (i + 1) * BLOCK),
        compiler_params=PARAMS,
    )(*([q, *parts] + [table] * needs_table))


def call_flags(stages, table, blocks_here):
    entries = sum(count for pieces in stages for _, _, count in pieces) * blocks_here
    return pl.pallas_call(
        functools.partial(flags_stage, stages, blocks_here),
        in_specs=[SMEM_SPEC],
        out_specs=VMEM_SPEC,
        out_shape=jax.ShapeDtypeStruct((-(-entries // 8) * 8, TILE), jnp.float32),
        compiler_params=PARAMS,
        name="flags",
    )(table)


def call_arrival(source, row_of, arrays, flags, state, last=False):
    rows_per_block = state[0][0].shape[1]
    rows = rows_per_block * len(state)
    dtype = arrays[0].dtype
    keys = sum(a.shape[1] for a in arrays)
    scratch = [pltpu.VMEM((keys, 2 * DH), dtype), pltpu.VMEM((DH + ONES, keys), dtype)]
    if last:
        scratch = [pltpu.VMEM((rows, DH), dtype), *scratch, pltpu.SemaphoreType.DMA((rows // min(TILE, keys),))]
    args = [] if row_of is None else [flags]
    args += [*[a for block in state for a in block], *arrays]
    out = pl.pallas_call(
        functools.partial(arrival_stage, source, row_of, len(arrays), len(state), last),
        in_specs=[VMEM_SPEC] * len(args),
        out_specs=ANY_SPEC if last else [VMEM_SPEC] * (2 * len(state)),
        out_shape=jax.ShapeDtypeStruct((rows, DH), dtype) if last else state_shapes(rows_per_block) * len(state),
        scratch_shapes=scratch,
        cost_estimate=cost(rows, keys),
        compiler_params=PARAMS,
    )(*args)
    return out if last else [(out[2 * i], out[2 * i + 1], block[2]) for i, block in enumerate(state)]


def shards(queries, key_states, value_states, block_table):
    tokens = queries.shape[0]
    per_head = queries.shape[2]
    blocks_here = tokens // BLOCK
    context_count = lax.axis_size("ctx")
    cores = lax.axis_size("qsub")
    per_core = blocks_here // cores
    core = lax.axis_index("qsub")
    q = queries.reshape(tokens * per_head, DH)
    k = key_states.reshape(tokens, DH)
    v = value_states.reshape(tokens, DH)

    part = per_core * BLOCK
    packed = jnp.stack(
        [lax.dynamic_slice_in_dim(k, core * part, part), lax.dynamic_slice_in_dim(v, core * part, part)]
    )

    def swapped(arrived):
        return [
            lax.ppermute(arrived, "qsub", [(c, (c + shift) % cores) for c in range(cores)])
            for shift in range(1, cores)
        ]

    def hop(block, route):
        return lax.ppermute(block, "ctx", route)

    def local(i, parts):
        return call_local(i, q, parts, block_table, per_head)

    def pieces_of(kind, source):
        pieces = []
        for shift in range(cores):
            base = lambda me, core, shift=shift: jnp.where(
                source(me) < 0, -1, source(me) * blocks_here + lax.rem(core - shift + cores, cores) * per_core
            )
            pieces.append((kind, base, per_core))
        return pieces

    def flags_of(stages):
        return call_flags(stages, block_table, blocks_here)

    if context_count == 4:
        ring = [0, 1, 2, 3]
        after = {d: ring[(ring.index(d) + 1) % 4] for d in ring}
        before = {d: ring[(ring.index(d) - 1) % 4] for d in ring}
        forward = [(d, after[d]) for d in range(4)]
        backward = [(d, before[d]) for d in range(4)]
        origins = [before, after, {0: 3, 1: 2, 2: 0, 3: 1}]
        sources = [
            lambda me, pairs=pairs: reduce(lambda acc, d: jnp.where(me == d, pairs[d], acc), range(4), jnp.int32(0))
            for pairs in origins
        ]
        tabled = [any(o < d and (o + 1) * blocks_here > SINKS for d, o in pairs.items()) for pairs in origins]
        row_of, listed = [], []
        for n in range(3):
            row_of.append(len(listed) * per_core * cores * blocks_here if tabled[n] else None)
            if tabled[n]:
                listed.append(pieces_of("all", sources[n]))

        one = hop(packed, forward)
        parts = [packed, *swapped(packed)]
        state = [local(0, parts)]
        other = hop(packed, backward)
        flags = flags_of(listed) if listed else None
        state += [local(i, parts) for i in range(1, blocks_here)]
        one, state = lax.optimization_barrier((one, state))
        swap = swapped(one)
        route = [(c, (c + 1) % cores) for c in range(cores)]
        route += [(a * cores + c, b * cores + c) for a, b in ((1, 2), (2, 3), (3, 1)) for c in range(cores)]
        two = lax.ppermute(one, ("ctx", "qsub"), route)
        state = call_arrival(sources[0], row_of[0], [one, *swap], flags, state)
        for n, arrived in ((1, other), (2, two)):
            arrived, state = lax.optimization_barrier((arrived, state))
            swap = swapped(arrived)
            row = row_of[n]
            state = call_arrival(sources[n], row, [arrived], flags, state)
            row = None if row is None else row + per_core * blocks_here
            state = call_arrival(sources[n], row, swap, flags, state, last=n == 2)
        attended = state
    else:
        parts = [packed, *swapped(packed)]
        state = [local(i, parts) for i in range(blocks_here)]
        wanted = []
        for level in range(LEVELS):
            amount = max(2**level // blocks_here, 1)
            if amount < context_count and amount not in wanted:
                wanted.append(amount)
        roots = -(-SINKS // blocks_here)
        position = lax.axis_index("ctx")
        shared = [
            lax.psum(jnp.where(position == root, packed, jnp.zeros_like(packed)), "ctx") for root in range(roots)
        ]
        stages = []
        moved, reached = packed, 0
        for amount in wanted:
            step = amount - reached
            moved = hop(moved, [(d, d + step) for d in range(context_count - step)])
            reached = amount
            stages.append((moved, "level", lambda me, amount=amount: jnp.maximum(me - amount, -1)))
        for root, arrived in enumerate(shared):
            stages.append((arrived, "sink", lambda me, root=root: jnp.int32(root)))
        flags = flags_of([pieces_of(kind, source) for _, kind, source in stages])
        for n, (arrived, _, source) in enumerate(stages):
            row = n * per_core * cores * blocks_here
            arrays = [arrived, *swapped(arrived)]
            state = call_arrival(source, row, arrays, flags, state, last=n == len(stages) - 1)
        attended = state
    return attended.reshape(tokens, 1, per_head, DH)


def solution(mesh):
    placed = (
        P(("groups", "ctx"), "head", "qsub", None),
        P(("groups", "ctx"), "head", None),
        P(("groups", "ctx"), "head", None),
        P(("groups", "ctx"), None),
    )

    return jax.shard_map(
        shards,
        mesh=mesh,
        in_specs=placed,
        out_specs=P(("groups", "ctx"), "head", "qsub", None),
        check_vma=False,
    )
```

```python
import functools
import math
from functools import reduce

import jax
import jax.numpy as jnp
from jax import lax
from jax.experimental import pallas as pl
from jax.experimental.pallas import tpu as pltpu
from jax.sharding import PartitionSpec as P


DH = 128
BLOCK = 256
SINKS = 4
LEVELS = 7
TILE = 512
NEG = -1e30
BIG = 1e30
EXP2_SCALE = DH ** (-0.5) * math.log2(math.e)
ONES = 16


def named(table_ref, i, u):
    return reduce(lambda a, b: a | b, [table_ref[i, level] == u for level in range(LEVELS)])


def counts_of(kind, table_ref, i, block, u, first_here, blocks_here):
    before = (u >= 0) & (u < block)
    elsewhere = (u < first_here) | (u >= first_here + blocks_here)
    if kind == "all":
        return before & elsewhere & ((u < SINKS) | named(table_ref, i, u))
    if kind == "sink":
        return before & elsewhere & (u < SINKS)
    return before & elsewhere & (u >= SINKS) & named(table_ref, i, u)


def split_queries(q):
    scaled = q.astype(jnp.float32) * EXP2_SCALE
    high = scaled.astype(jnp.bfloat16)
    low = (scaled - high.astype(jnp.float32)).astype(jnp.bfloat16)
    return jnp.concatenate([high, low], axis=1)


def scores(k, q):
    return lax.dot_general(k, q, (((1,), (1,)), ((), ())), preferred_element_type=jnp.float32)


def top_of(s):
    return jnp.max(s, axis=0, keepdims=True)


def weights(s, shift):
    return jnp.exp2(s - shift).astype(jnp.bfloat16)


def keep_state(acc_ref, stat_ref, cols, acc, highest, total):
    acc_ref[:, cols] = acc
    stat_ref[:8, cols] = jnp.broadcast_to(highest, total.shape)
    stat_ref[8:, cols] = total


def local_stage(i, per_head, cores, q_ref, *refs):
    refs = list(refs)
    parts = [refs.pop(0) for _ in range(cores)]
    table_ref = refs.pop(0) if len(refs) == 7 else None
    acc_ref, stat_ref, split_ref, k_ref, v_ref, vt_ref = refs
    core = lax.axis_index("qsub")
    part = parts[0].shape[1]
    for shift, ref in enumerate(parts):
        at = pl.ds(pl.multiple_of(lax.rem(core - shift + cores, cores) * part, part), part)
        k_ref[at, :DH] = ref[0]
        k_ref[at, DH:] = ref[0]
        v_ref[at, :] = ref[1]
    keys = (i + 1) * BLOCK
    vt_ref[:DH, :] = v_ref[:keys, :].T
    vt_ref[DH:, :] = jnp.ones((ONES, keys), vt_ref.dtype)
    rows_per_block = BLOCK * per_head
    tokens = TILE // per_head
    first_here = lax.axis_index("ctx") * (k_ref.shape[0] // BLOCK)
    for t in range(rows_per_block // TILE):
        q = split_queries(q_ref[pl.ds(i * rows_per_block + t * TILE, TILE), :])
        split_ref[pl.ds(t * TILE, TILE), :] = q
        edge = i * BLOCK + t * tokens
        items = []
        for j in range(i):
            s = scores(k_ref[pl.ds(j * BLOCK, BLOCK), :], q)
            if j < i - 1:
                u = first_here + j
                s = jnp.where((u < SINKS) | named(table_ref, i, u), s, NEG)
            items.append(s)
        if t:
            items.append(scores(k_ref[pl.ds(i * BLOCK, t * tokens), :], q))
        token = lax.broadcasted_iota(jnp.int32, (tokens, TILE), 1) // per_head
        mask = lax.broadcasted_iota(jnp.int32, (tokens, TILE), 0) <= token
        items.append(jnp.where(mask, scores(k_ref[pl.ds(edge, tokens), :], q), NEG))
        highest = reduce(jnp.maximum, [top_of(s) for s in items])
        w = jnp.concatenate([weights(s, highest) for s in items], axis=0)
        sums = jnp.dot(vt_ref[:, : edge + tokens], w, preferred_element_type=jnp.float32)
        keep_state(acc_ref, stat_ref, pl.ds(t * TILE, TILE), sums[:DH], highest, sums[DH : DH + 8])


def flags_stage(stages, blocks_here, table_ref, flags_ref):
    me, core = lax.axis_index("ctx"), lax.axis_index("qsub")
    first_here = me * blocks_here
    at = 0
    for pieces in stages:
        for kind, base, count in pieces:
            start = base(me, core)
            for j in range(count):
                u = jnp.where(start < 0, -1, start + j)
                for i in range(blocks_here):
                    counts = counts_of(kind, table_ref, i, first_here + i, u, first_here, blocks_here)
                    flags_ref[at : at + 1, :] = jnp.full((1, TILE), jnp.where(counts, 0.0, BIG), jnp.float32)
                    at += 1


def arrival_stage(source, row_of, operands, blocks_here, last, early, *refs):
    refs = list(refs)
    flags_ref = None if row_of is None else refs.pop(0)
    state_in = [(refs.pop(0), refs.pop(0), refs.pop(0)) for _ in range(blocks_here)]
    arrived = [refs.pop(0) for _ in range(operands)]
    if last:
        if early:
            refs.pop(0)
        out_hbm, out_ref, k_ref, vt_ref, sems = refs
    else:
        state_out = [(refs.pop(0), refs.pop(0)) for _ in range(blocks_here)]
        if early:
            out_hbm, out_ref, k_ref, vt_ref, sems = refs
        else:
            k_ref, vt_ref = refs
    me = lax.axis_index("ctx")
    origin = source(me)
    some = (origin >= 0) & (origin < me)
    key_blocks = k_ref.shape[0] // BLOCK
    rows_per_block = state_in[0][0].shape[1]
    tile = min(TILE, k_ref.shape[0])
    depth = 2 * TILE // tile
    per_block = rows_per_block // tile
    tiles = per_block * blocks_here

    def place(t):
        return t // per_block, pl.ds(t % per_block * tile, tile)

    def finish(t, acc, highest, total):
        i, cols = place(t)
        if not last:
            keep_state(*state_out[i], cols, acc, highest, total)
            return
        write(t, acc, total)

    def write(t, acc, total):
        rows = pl.ds(t * tile, tile)
        out_ref[rows, :] = (acc * (1.0 / total[:1])).astype(out_ref.dtype).T
        pltpu.make_async_copy(out_ref.at[rows], out_hbm.at[rows], sems.at[t]).start()

    @pl.when(some)
    def _():
        at = 0
        for ref in arrived:
            span = pl.ds(at, ref.shape[1])
            k_ref[span, :DH] = ref[0]
            k_ref[span, DH:] = ref[0]
            vt_ref[:DH, span] = ref[1].T
            at += ref.shape[1]
        vt_ref[DH:, :] = jnp.ones((ONES, at), vt_ref.dtype)
        k, vt = k_ref[...], vt_ref[...]

        def begin(t):
            i, cols = place(t)
            return scores(k, state_in[i][2][cols, :])

        raw = [begin(t) for t in range(min(depth, tiles))]
        for t in range(tiles):
            if t + depth < tiles:
                raw.append(begin(t + depth))
            s = raw.pop(0)
            i, cols = place(t)
            acc_in, stat_in, _ = state_in[i]
            before = stat_in[:1, cols]
            if row_of is None:
                highest = jnp.maximum(before, top_of(s))
                w = weights(s, highest)
            else:
                parts = [s[j * BLOCK : (j + 1) * BLOCK] for j in range(key_blocks)]
                at = [row_of + j * blocks_here + i for j in range(key_blocks)]
                off = [flags_ref[n : n + 1, :tile] for n in at]
                highest = reduce(jnp.maximum, [top_of(part) - o for part, o in zip(parts, off)], before)
                w = jnp.concatenate([weights(part, highest + o) for part, o in zip(parts, off)], axis=0)
            sums = jnp.dot(vt, w, preferred_element_type=jnp.float32)
            keep = jnp.exp2(before - highest)
            finish(t, acc_in[:, cols] * keep + sums[:DH], highest, stat_in[8:, cols] * keep + sums[DH : DH + 8])

    def arrive():
        for t in range(tiles):
            rows = pl.ds(t * tile, tile)
            pltpu.make_async_copy(out_ref.at[rows], out_hbm.at[rows], sems.at[t]).wait()

    if last and early:
        pl.when(some)(arrive)
        return

    @pl.when(jnp.logical_not(some))
    def _():
        for t in range(tiles):
            i, cols = place(t)
            acc_in, stat_in, _ = state_in[i]
            if early:
                write(t, acc_in[:, cols], stat_in[8:, cols])
            else:
                finish(t, acc_in[:, cols], stat_in[:1, cols], stat_in[8:, cols])
        if early:
            arrive()

    if last:
        arrive()


VMEM_SPEC = pl.BlockSpec(memory_space=pltpu.VMEM)
SMEM_SPEC = pl.BlockSpec(memory_space=pltpu.SMEM)
ANY_SPEC = pl.BlockSpec(memory_space=pl.ANY)
PARAMS = pltpu.CompilerParams(vmem_limit_bytes=16 << 20)


def state_shapes(rows):
    return [jax.ShapeDtypeStruct((DH, rows), jnp.float32), jax.ShapeDtypeStruct((16, rows), jnp.float32)]


def cost(rows, keys):
    return pl.CostEstimate(flops=4 * rows * keys * DH, bytes_accessed=8 * rows * DH, transcendentals=rows * keys)


def call_local(i, q, parts, table, per_head):
    tokens = sum(a.shape[1] for a in parts)
    rows = BLOCK * per_head
    needs_table = i > 1
    return pl.pallas_call(
        functools.partial(local_stage, i, per_head, len(parts)),
        in_specs=[VMEM_SPEC] * (1 + len(parts)) + [SMEM_SPEC] * needs_table,
        out_specs=[VMEM_SPEC] * 3,
        out_shape=[*state_shapes(rows), jax.ShapeDtypeStruct((rows, 2 * DH), q.dtype)],
        scratch_shapes=[
            pltpu.VMEM((tokens, 2 * DH), q.dtype),
            pltpu.VMEM((tokens, DH), q.dtype),
            pltpu.VMEM((DH + ONES, (i + 1) * BLOCK), q.dtype),
        ],
        cost_estimate=cost(rows, (i + 1) * BLOCK),
        compiler_params=PARAMS,
    )(*([q, *parts] + [table] * needs_table))


def call_flags(stages, table, blocks_here):
    entries = sum(count for pieces in stages for _, _, count in pieces) * blocks_here
    return pl.pallas_call(
        functools.partial(flags_stage, stages, blocks_here),
        in_specs=[SMEM_SPEC],
        out_specs=VMEM_SPEC,
        out_shape=jax.ShapeDtypeStruct((-(-entries // 8) * 8, TILE), jnp.float32),
        compiler_params=PARAMS,
        name="flags",
    )(table)


def call_arrival(source, row_of, arrays, flags, state, last=False, early=False, written=None):
    rows_per_block = state[0][0].shape[1]
    rows = rows_per_block * len(state)
    dtype = arrays[0].dtype
    keys = sum(a.shape[1] for a in arrays)
    scratch = [pltpu.VMEM((keys, 2 * DH), dtype), pltpu.VMEM((DH + ONES, keys), dtype)]
    early = early or written is not None
    if last or early:
        scratch = [pltpu.VMEM((rows, DH), dtype), *scratch, pltpu.SemaphoreType.DMA((rows // min(TILE, keys),))]
    args = [] if row_of is None else [flags]
    args += [*[a for block in state for a in block], *arrays]
    in_specs = [VMEM_SPEC] * len(args)
    output = jax.ShapeDtypeStruct((rows, DH), dtype)
    out_shape, out_specs = [], []
    if not last:
        out_shape, out_specs = state_shapes(rows_per_block) * len(state), [VMEM_SPEC] * (2 * len(state))
    if last or early:
        out_shape, out_specs = [*out_shape, output], [*out_specs, ANY_SPEC]
    aliases = {}
    if written is not None:
        aliases = {len(args): 0}
        args, in_specs = [*args, written], [*in_specs, ANY_SPEC]
    out = pl.pallas_call(
        functools.partial(arrival_stage, source, row_of, len(arrays), len(state), last, early),
        in_specs=in_specs,
        out_specs=out_specs,
        out_shape=out_shape,
        scratch_shapes=scratch,
        input_output_aliases=aliases,
        cost_estimate=cost(rows, keys),
        compiler_params=PARAMS,
    )(*args)
    if last:
        return out[0]
    state = [(out[2 * i], out[2 * i + 1], block[2]) for i, block in enumerate(state)]
    return (state, out[-1]) if early else state


def shards(queries, key_states, value_states, block_table):
    tokens = queries.shape[0]
    per_head = queries.shape[2]
    blocks_here = tokens // BLOCK
    context_count = lax.axis_size("ctx")
    cores = lax.axis_size("qsub")
    per_core = blocks_here // cores
    core = lax.axis_index("qsub")
    q = queries.reshape(tokens * per_head, DH)
    k = key_states.reshape(tokens, DH)
    v = value_states.reshape(tokens, DH)

    part = per_core * BLOCK
    packed = jnp.stack(
        [lax.dynamic_slice_in_dim(k, core * part, part), lax.dynamic_slice_in_dim(v, core * part, part)]
    )

    def swapped(arrived):
        return [
            lax.ppermute(arrived, "qsub", [(c, (c + shift) % cores) for c in range(cores)])
            for shift in range(1, cores)
        ]

    def hop(block, route):
        return lax.ppermute(block, "ctx", route)

    def local(i, parts):
        return call_local(i, q, parts, block_table, per_head)

    def pieces_of(kind, source):
        pieces = []
        for shift in range(cores):
            base = lambda me, core, shift=shift: jnp.where(
                source(me) < 0, -1, source(me) * blocks_here + lax.rem(core - shift + cores, cores) * per_core
            )
            pieces.append((kind, base, per_core))
        return pieces

    def flags_of(stages):
        return call_flags(stages, block_table, blocks_here)

    if context_count == 4:
        ring = [0, 1, 2, 3]
        after = {d: ring[(ring.index(d) + 1) % 4] for d in ring}
        before = {d: ring[(ring.index(d) - 1) % 4] for d in ring}
        forward = [(d, after[d]) for d in range(4)]
        backward = [(d, before[d]) for d in range(4)]
        origins = [before, after, {0: 3, 1: 2, 2: 0, 3: 1}]
        sources = [
            lambda me, pairs=pairs: reduce(lambda acc, d: jnp.where(me == d, pairs[d], acc), range(4), jnp.int32(0))
            for pairs in origins
        ]
        tabled = [any(o < d and (o + 1) * blocks_here > SINKS for d, o in pairs.items()) for pairs in origins]
        row_of, listed = [], []
        for n in range(3):
            row_of.append(len(listed) * per_core * cores * blocks_here if tabled[n] else None)
            if tabled[n]:
                listed.append(pieces_of("all", sources[n]))

        one = hop(packed, forward)
        parts = [packed, *swapped(packed)]
        state = [local(0, parts)]
        other = hop(packed, backward)
        flags = flags_of(listed) if listed else None
        state += [local(i, parts) for i in range(1, blocks_here)]
        one, state = lax.optimization_barrier((one, state))
        swap = swapped(one)
        route = [(c, (c + 1) % cores) for c in range(cores)]
        route += [(a * cores + c, b * cores + c) for a, b in ((1, 2), (2, 3), (3, 1)) for c in range(cores)]
        two = lax.ppermute(one, ("ctx", "qsub"), route)
        state = call_arrival(sources[0], row_of[0], [one, *swap], flags, state)
        for n, arrived in ((1, other), (2, two)):
            arrived, state = lax.optimization_barrier((arrived, state))
            swap = swapped(arrived)
            row = row_of[n]
            written = None
            state = call_arrival(sources[n], row, [arrived], flags, state, early=n == 2)
            if n == 2:
                state, written = state
            row = None if row is None else row + per_core * blocks_here
            state = call_arrival(sources[n], row, swap, flags, state, last=n == 2, written=written)
        attended = state
    else:
        parts = [packed, *swapped(packed)]
        state = [local(i, parts) for i in range(blocks_here)]
        wanted = []
        for level in range(LEVELS):
            amount = max(2**level // blocks_here, 1)
            if amount < context_count and amount not in wanted:
                wanted.append(amount)
        roots = -(-SINKS // blocks_here)
        position = lax.axis_index("ctx")
        shared = [
            lax.psum(jnp.where(position == root, packed, jnp.zeros_like(packed)), "ctx") for root in range(roots)
        ]
        stages = []
        moved, reached = packed, 0
        for amount in wanted:
            step = amount - reached
            moved = hop(moved, [(d, d + step) for d in range(context_count - step)])
            reached = amount
            stages.append((moved, "level", lambda me, amount=amount: jnp.maximum(me - amount, -1)))
        for root, arrived in enumerate(shared):
            stages.append((arrived, "sink", lambda me, root=root: jnp.int32(root)))
        flags = flags_of([pieces_of(kind, source) for _, kind, source in stages])
        for n, (arrived, _, source) in enumerate(stages):
            row = n * per_core * cores * blocks_here
            arrays = [arrived, *swapped(arrived)]
            state = call_arrival(source, row, arrays, flags, state, last=n == len(stages) - 1)
        attended = state
    return attended.reshape(tokens, 1, per_head, DH)


def solution(mesh):
    placed = (
        P(("groups", "ctx"), "head", "qsub", None),
        P(("groups", "ctx"), "head", None),
        P(("groups", "ctx"), "head", None),
        P(("groups", "ctx"), None),
    )

    return jax.shard_map(
        shards,
        mesh=mesh,
        in_specs=placed,
        out_specs=P(("groups", "ctx"), "head", "qsub", None),
        check_vma=False,
    )
```
